32 devices in a mesh: fsdp: 8 (over z, x), sp: 4 (over y, core).
Axes of the slice: x: 2, y: 2, z: 4, core: 2. Of those that a mesh axis runs over, the one named last changes fastest.
Arguments:
- hidden_in: bfloat16 [32, 1024, 768], P('fsdp', 'sp'), may hold values from -6 to 6
- doc_starts: int32 [32, 4], P('fsdp'), may hold values from 0 to 1023, as said below
- w_qkv: bfloat16 [768, 2304], P('fsdp'), may hold values from -0.21875 to 0.21875
- query_bias: bfloat16 [768], P('fsdp'), may hold values from -3 to 3
- value_bias: bfloat16 [768], P('fsdp'), may hold values from -3 to 3
- w_out: bfloat16 [768, 768], P('fsdp'), may hold values from -1.75 to 1.75
- out_bias: bfloat16 [768], P('fsdp'), may hold values from -2 to 2
- norm1_gain: bfloat16 [768], P('fsdp'), may hold values from 0.5 to 1.5
- norm1_bias: bfloat16 [768], P('fsdp'), may hold values from -2 to 2
- w_up: bfloat16 [768, 3072], P('fsdp'), may hold values from -0.21875 to 0.21875
- up_bias: bfloat16 [3072], P('fsdp'), may hold values from -3 to 3
- w_down: bfloat16 [3072, 768], P('fsdp'), may hold values from -0.21875 to 0.21875
- down_bias: bfloat16 [768], P('fsdp'), may hold values from -2 to 2
- norm2_gain: bfloat16 [768], P('fsdp'), may hold values from 0.5 to 1.5
- norm2_bias: bfloat16 [768], P('fsdp'), may hold values from -2 to 2
- cotangent: bfloat16 [32, 1024, 768], P('fsdp', 'sp'), may hold values from -6 to 6
Outputs:
- layer_out: bfloat16 [32, 1024, 768], P('fsdp', 'sp')
- grad_input: bfloat16 [32, 1024, 768], P('fsdp', 'sp')
- grad_w_qkv: float32 [768, 2304], P('fsdp')
- grad_query_bias: float32 [768], P('fsdp')
- grad_value_bias: float32 [768], P('fsdp')
- grad_w_out: float32 [768, 768], P('fsdp')
- grad_out_bias: float32 [768], P('fsdp')
- grad_norm1_gain: float32 [768], P('fsdp')
- grad_norm1_bias: float32 [768], P('fsdp')
- grad_w_up: float32 [768, 3072], P('fsdp')
- grad_up_bias: float32 [3072], P('fsdp')
- grad_w_down: float32 [3072, 768], P('fsdp')
- grad_down_bias: float32 [768], P('fsdp')
- grad_norm2_gain: float32 [768], P('fsdp')
- grad_norm2_bias: float32 [768], P('fsdp')
The draws below stay inside these ranges and needn't reach their ends.
Inputs may be any that keep to these rules, and one draw needn't show every extreme that they name: `doc_starts`: in each row entry 0 is 0 and the entries rise strictly; document j of a sequence spans its positions from entry j up to the next entry, or to position 1023.
All inputs are finite; a program needn't handle non-finite values.
Results may differ from the reference program's by a relative error of at most 0.018.
Values may be sent and summed in bfloat16 or wider, within the bound.
No kernel may reach another device: no remote copies, remote signals or barrier semaphores. Data moves between devices by JAX's collectives and lax.ppermute only.
A program may use at most 192 MiB of HBM per device.

```python
import jax
import jax.numpy as jnp
from jax import lax

D = 768
H = 12
HD = 64
FF = 3072
SEQ = 1024
NDOC = 4
SEQS = 32


def draw_doc_starts(key, part):
    row_keys = jax.random.split(jax.random.fold_in(key, 17), SEQS)
    row_index = jnp.arange(SEQS, dtype=jnp.int32)

    def one_row(row_key, index):
        picked = jnp.sort(jax.random.permutation(row_key, SEQ - 1)[:NDOC - 1] + 1).astype(jnp.int32)
        top_value = jnp.where(index == 0, jnp.int32(SEQ - 1), picked[NDOC - 2])
        picked = picked.at[NDOC - 2].set(top_value)
        return jnp.concatenate([jnp.zeros((1,), jnp.int32), picked])
    return jax.vmap(one_row)(row_keys, row_index)


def strengthened(values, key, source, target, blocks, factor):
    def block_of(dim):
        return (jnp.arange(values.shape[dim]) // (values.shape[dim] // blocks)).reshape((-1,) + (1,) * (values.ndim - 1 - dim))

    near = jax.random.permutation(key, blocks)[block_of(target)]
    far = (block_of(target) + blocks // 2) % blocks
    return jnp.where((block_of(source) == near) | (block_of(source) == far), factor * values, values)


def block_scale(stream_key, extent, cuts, smallest, largest):
    def one(position, parts):
        steps = jax.random.uniform(jax.random.fold_in(jax.random.fold_in(stream_key, 6), position), (parts,), jnp.float32, smallest / len(cuts), largest / len(cuts))
        return jnp.repeat(jnp.exp(steps), extent[position] // parts).reshape((-1,) + (1,) * (len(extent) - position - 1))

    level = one(*cuts[0])
    for cut in cuts[1:]:
        level = level * one(*cut)
    return level


def scatter_about(own_key, shape, deviation, most, cuts=(), kind=jnp.bfloat16):
    entries = deviation * jax.random.normal(own_key, shape, jnp.float32)
    if cuts:
        entries = entries * block_scale(own_key, shape, cuts, -0.22, 0.18)
    return jnp.clip(entries, -most, most).astype(kind)


def gaussian_with(rng, shape, spread, limit, pieces, heavy, kind=jnp.bfloat16):
    drawn = spread * jax.random.normal(rng, shape, jnp.float32)
    if pieces:
        drawn = drawn * block_scale(rng, shape, pieces, -0.22, 0.18)
    return jnp.clip(strengthened(drawn, jax.random.fold_in(rng, 3), *heavy), -limit, limit).astype(kind)


def setup_inputs(seed: int = 0) -> dict:
    streams_of = jax.random.split(jax.random.key(seed), 17)
    hidden_in = gaussian_with(streams_of[0], (SEQS, SEQ, D), 1.0, 6.0, ((0, 8), (1, 4)), (0, 2, 8, 2.0))
    doc_starts = draw_doc_starts(jax.random.fold_in(streams_of[16], 71), 0)
    w_qkv = scatter_about(streams_of[2], (D, 3 * D), D ** -0.5, 0.21875, ((0, 8),))
    query_bias = scatter_about(streams_of[3], (D,), 0.5, 3.0, ((0, 8),))
    value_bias = scatter_about(streams_of[4], (D,), 0.5, 3.0, ((0, 8),))
    w_out = scatter_about(streams_of[5], (D, D), (max(D // 64, 1)) ** -0.5, 1.75, ((0, 8),))
    out_bias = scatter_about(streams_of[6], (D,), 0.3, 2.0, ((0, 8),))
    norm1_gain = jnp.clip(1.0 + 0.1 * jax.random.normal(streams_of[7], (D,), jnp.float32), 0.5, 1.5).astype(jnp.bfloat16)
    norm1_bias = scatter_about(streams_of[8], (D,), 0.3, 2.0, ((0, 8),))
    w_up = scatter_about(streams_of[9], (D, FF), D ** -0.5, 0.21875, ((0, 8),))
    up_bias = scatter_about(streams_of[10], (FF,), 0.5, 3.0, ((0, 8),))
    w_down = scatter_about(streams_of[11], (FF, D), (FF // 4) ** -0.5, 0.21875, ((0, 8),))
    down_bias = scatter_about(streams_of[12], (D,), 0.3, 2.0, ((0, 8),))
    norm2_gain = jnp.clip(1.0 + 0.1 * jax.random.normal(streams_of[13], (D,), jnp.float32), 0.5, 1.5).astype(jnp.bfloat16)
    norm2_bias = scatter_about(streams_of[14], (D,), 0.3, 2.0, ((0, 8),))
    cotangent = gaussian_with(streams_of[15], (SEQS, SEQ, D), 1.0, 6.0, ((0, 8), (1, 4)), (0, 2, 8, 2.0))
    return dict(hidden_in=hidden_in, doc_starts=doc_starts, w_qkv=w_qkv, query_bias=query_bias, value_bias=value_bias, w_out=w_out, out_bias=out_bias, norm1_gain=norm1_gain, norm1_bias=norm1_bias, w_up=w_up, up_bias=up_bias, w_down=w_down, down_bias=down_bias, norm2_gain=norm2_gain, norm2_bias=norm2_bias, cotangent=cotangent)


@jax.custom_vjp
def low(v):
    return lax.optimization_barrier(v.astype(jnp.bfloat16)).astype(jnp.float32)

@jax.custom_vjp
def low_back(v):
    return v

def low_keep(v):
    return (low(v), None)

def low_pass(kept, grad):
    return (grad,)

def back_keep(v):
    return (v, None)

def back_low(kept, grad):
    return (low(grad),)
low.defvjp(low_keep, low_pass)
low_back.defvjp(back_keep, back_low)
NORM_EPS = 1e-05
MASK_VALUE = -1000000000.0

def normalize(values, gain, shift):
    centred = values - lax.optimization_barrier(jnp.mean(values, -1, keepdims=True))
    variance = lax.optimization_barrier(jnp.mean(centred * centred, -1, keepdims=True))
    return centred * lax.rsqrt(variance + NORM_EPS) * gain + shift

def layer_forward(params, token_rows, segment_ids):
    w_qkv, query_bias, value_bias, w_out, out_bias, norm1_gain, norm1_bias, w_up, up_bias, w_down, down_bias, norm2_gain, norm2_bias = params
    highest = lax.Precision.HIGHEST
    merged_proj = jnp.dot(token_rows, w_qkv, precision=highest)
    queries = low_back(low(merged_proj[:, :D] + query_bias))
    key_rows = low_back(low(merged_proj[:, D:2 * D]))
    value_rows = low_back(low(merged_proj[:, 2 * D:] + value_bias))
    score_scale = HD ** (-0.5)
    query_heads = queries.reshape(SEQ, H, HD)
    key_heads = key_rows.reshape(SEQ, H, HD)
    value_heads = value_rows.reshape(SEQ, H, HD)
    scores = low_back(jnp.einsum('qhd,khd->hqk', query_heads, key_heads, precision=highest) * score_scale)
    same_doc = segment_ids[:, None] == segment_ids[None, :]
    scores = jnp.where(same_doc[None], scores, MASK_VALUE)
    probs_low = low(jax.nn.softmax(scores, axis=-1))
    context = jnp.einsum('hqk,khd->qhd', probs_low, value_heads, precision=highest).reshape(SEQ, D)
    context = low_back(low(context))
    attn_out = low_back(jnp.dot(context, w_out, precision=highest) + out_bias)
    first_normalized1 = normalize(token_rows + attn_out, norm1_gain, norm1_bias)
    pre_act = low_back(jnp.dot(low(first_normalized1), w_up, precision=highest) + up_bias)
    activated = low(jax.nn.gelu(pre_act, approximate=False))
    ffn_out = low_back(jnp.dot(activated, w_down, precision=highest) + down_bias)
    return normalize(first_normalized1 + ffn_out, norm2_gain, norm2_bias)

def reference(hidden_in, doc_starts, w_qkv, query_bias, value_bias, w_out, out_bias, norm1_gain, norm1_bias, w_up, up_bias, w_down, down_bias, norm2_gain, norm2_bias, cotangent):
    params = tuple((weight.astype(jnp.float32) for weight in (w_qkv, query_bias, value_bias, w_out, out_bias, norm1_gain, norm1_bias, w_up, up_bias, w_down, down_bias, norm2_gain, norm2_bias)))
    positions = jnp.arange(SEQ, dtype=jnp.int32)

    def one_sequence(running, inputs):
        token_rows, starts, grad_rows = inputs
        segment_ids = lax.optimization_barrier(jnp.sum((positions[:, None] >= starts[None, :]).astype(jnp.int32), -1))
        result, pullback = jax.vjp(lambda weights, rows_in: layer_forward(weights, rows_in, segment_ids), params, token_rows)
        grad_params, grad_rows_in = pullback(grad_rows)
        running = jax.tree.map(lambda before, fresh: before + fresh, running, grad_params)
        return (running, (result.astype(jnp.bfloat16), grad_rows_in.astype(jnp.bfloat16)))
    zeroed = tuple((jnp.zeros_like(weight) for weight in params))
    totals, (outputs, grads_in) = lax.scan(one_sequence, zeroed, (hidden_in.astype(jnp.float32), doc_starts.astype(jnp.int32), cotangent.astype(jnp.float32)))
    return (outputs, grads_in, totals[0], totals[1], totals[2], totals[3], totals[4], totals[5], totals[6], totals[7], totals[8], totals[9], totals[10], totals[11], totals[12])
```

```python
import jax
import jax.numpy as jnp
from jax import lax
from jax.experimental import pallas as pl
from jax.experimental.pallas import tpu as pltpu
from jax.sharding import PartitionSpec as P

D = 768
H = 12
HD = 64
FF = 3072
SEQ = 1024
PAIRS = H // 2
EPS = 1e-05
MASKED = -1000000000.0
SCALE = HD ** (-0.5)
BF = jnp.bfloat16
F32 = jnp.float32
ROWS = 256
MIB = 1 << 20


ERFC = (
    0.2820844758103095,
    0.28240952292464144,
    0.24285408258103366,
    0.20367679547693512,
    -0.028968306758876145,
    0.2814702272328375,
    -0.49017537256556365,
    0.28601194065835034,
    -0.059363409284156475,
)


def nn(a, b):
    return lax.dot_general(a, b, (((1,), (0,)), ((), ())), preferred_element_type=F32)


def nt(a, b):
    return lax.dot_general(a, b, (((1,), (1,)), ((), ())), preferred_element_type=F32)


def tn(a, b):
    return lax.dot_general(a, b, (((0,), (0,)), ((), ())), preferred_element_type=F32)


def gelu_with_slope(x):
    z = jnp.abs(x) * 0.7071067811865476
    t = 1.0 / (1.0 + 0.5 * z)
    e = jnp.exp(-0.5 * (x * x))
    poly = jnp.full_like(t, 0.5 * ERFC[-1])
    for c in ERFC[-2::-1]:
        poly = poly * t + 0.5 * c
    tail = poly * t * e
    cdf = jnp.where(x >= 0, 1.0 - tail, tail)
    return x * cdf, cdf + x * (e * 0.3989422804014327)


def norm_rows(v):
    c = v - jnp.mean(v, -1, keepdims=True)
    r = lax.rsqrt(jnp.mean(c * c, -1, keepdims=True) + EPS)
    return c * r, r


def norm_rows_back(a, xhat, rstd):
    return rstd * (a - jnp.mean(a, -1, keepdims=True) - xhat * jnp.mean(a * xhat, -1, keepdims=True))


def piece_copies(pieces, cols, dst, sems, row_bit, col_bit):
    copies = []
    for rr in range(2):
        for rc in range(2):
            ref = pieces[rr][rc]
            count, nr, _ = ref.shape
            lo, nc = cols
            row0 = nr * lax.bitwise_xor(row_bit, rr)
            col0 = nc * lax.bitwise_xor(col_bit, rc)
            for j in range(count):
                copies.append(
                    pltpu.make_async_copy(
                        ref.at[j, :, pl.ds(lo, nc)],
                        dst.at[
                            pl.ds(pl.multiple_of(row0 + j * 2 * nr, nr), nr),
                            pl.ds(pl.multiple_of(col0, nc), nc),
                        ],
                        sems.at[(rr * 2 + rc) * count + j],
                    )
                )
    return copies


def whole_copies(ref, cols, dst, sems):
    lo, nc = cols
    return [pltpu.make_async_copy(ref.at[:, pl.ds(lo, nc)], dst, sems.at[0])]


def weight_copies(kind, refs, cols, full_cols, dst, sems, bits):
    if kind == "whole":
        return whole_copies(refs[0], full_cols, dst, sems)
    pieces = ((refs[0], refs[1]), (refs[2], refs[3]))
    return piece_copies(pieces, cols, dst, sems, bits[0], bits[1])


def start_all(copies):
    for c in copies:
        c.start()


def wait_all(copies):
    for c in copies:
        c.wait()


ANY = pl.BlockSpec(memory_space=pl.ANY)


def params(vmem=58):
    return pltpu.CompilerParams(
        dimension_semantics=("arbitrary",), vmem_limit_bytes=vmem * MIB
    )


def bits_of(me_ref):
    core = lax.bitwise_and(me_ref[0], 1)
    high = lax.shift_right_logical(me_ref[0], 1)
    return high, core


def project(me, x, weight, bias_row):
    kind, refs = weight
    n = 3 * D
    count = 4 * refs[0].shape[0] if kind == "pieces" else 1

    def kernel(me_ref, x_ref, b_ref, *rest):
        w_refs, (o_ref, w_ref, sems) = rest[:-3], rest[-3:]

        @pl.when(pl.program_id(0) == 0)
        def _():
            high, core = bits_of(me_ref)
            copies = weight_copies(kind, w_refs, (0, n // 2), (0, n), w_ref, sems, (high, core))
            start_all(copies)
            wait_all(copies)

        xv = x_ref[...]
        for lo in range(0, n, D):
            o_ref[:, lo : lo + D] = (
                nn(xv, w_ref[:, lo : lo + D]) + b_ref[:, lo : lo + D]
            ).astype(BF)

    rows = x.shape[0]
    return pl.pallas_call(
        kernel,
        grid_spec=pltpu.PrefetchScalarGridSpec(
            num_scalar_prefetch=1,
            grid=(rows // ROWS,),
            in_specs=[
                pl.BlockSpec((ROWS, D), lambda i, me: (i, 0)),
                pl.BlockSpec((1, n), lambda i, me: (0, 0)),
            ]
            + [ANY] * len(refs),
            out_specs=pl.BlockSpec((ROWS, n), lambda i, me: (i, 0)),
            scratch_shapes=[pltpu.VMEM((D, n), BF), pltpu.SemaphoreType.DMA((count,))],
        ),
        out_shape=jax.ShapeDtypeStruct((rows, n), BF),
        compiler_params=params(),
        name="project",
    )(me, x, bias_row, *refs)


def attend(qkv, seg_col, seg_row):
    chunk = 256

    def kernel(q_ref, k_ref, v_ref, sc_ref, sr_ref, o_ref, lse_ref):
        lane = lax.broadcasted_iota(jnp.int32, (1, 2 * HD), 1)
        k = k_ref[...]
        vt = v_ref[...].T
        seg_k = sc_ref[...]
        for c in range(SEQ // chunk):
            at = pl.ds(c * chunk, chunk)
            q = q_ref[at, :] * jnp.asarray(SCALE, BF)
            same = seg_k == sr_ref[:, at]
            outs = []
            for h in range(2):
                mine = (lane < HD) if h == 0 else (lane >= HD)
                s = nt(k, jnp.where(mine, q, jnp.zeros_like(q)))
                s = jnp.where(same, s, MASKED)
                m = jnp.max(s, 0, keepdims=True)
                p = jnp.exp(s - m)
                l = jnp.sum(p, 0, keepdims=True)
                lse_ref[0, h : h + 1, at] = m + jnp.log(l)
                o = nn(vt, p.astype(BF))
                outs.append(o[h * HD : (h + 1) * HD] * (1.0 / l))
            o_ref[at, :] = jnp.concatenate(outs, 0).T.astype(BF)

    spec = lambda off: pl.BlockSpec((SEQ, 2 * HD), lambda i: (0, i + off))
    full = lambda s: pl.BlockSpec(s, lambda i: (0,) * len(s))
    return pl.pallas_call(
        kernel,
        grid=(PAIRS,),
        in_specs=[spec(0), spec(PAIRS), spec(2 * PAIRS), full((SEQ, 1)), full((1, SEQ))],
        out_specs=[spec(0), pl.BlockSpec((1, 8, SEQ), lambda i: (i, 0, 0))],
        out_shape=[
            jax.ShapeDtypeStruct((SEQ, D), BF),
            jax.ShapeDtypeStruct((PAIRS, 8, SEQ), F32),
        ],
        compiler_params=params(),
        name="attend",
    )(qkv, qkv, qkv, seg_col, seg_row)


def attend_back(qkv, context, grad_context, lse, seg_col, seg_row):
    chunk = 256

    def kernel(q_ref, k_ref, v_ref, o_ref, g_ref, lse_ref, sc_ref, sr_ref,
               dq_ref, dk_ref, dv_ref, sum_ref, acc_ref, kt_ref):
        lane = lax.broadcasted_iota(jnp.int32, (1, 2 * HD), 1)
        first = lane < HD
        q = q_ref[...] * jnp.asarray(SCALE, BF)
        g = g_ref[...]
        zero = jnp.zeros_like(q)
        prod = (g.astype(F32) * o_ref[...].astype(F32)).T
        inner = [jnp.sum(prod[h * HD : (h + 1) * HD], 0, keepdims=True) for h in range(2)]
        qm = [jnp.where(first, q, zero), jnp.where(first, zero, q)]
        gm = [jnp.where(first, g, zero), jnp.where(first, zero, g)]
        seg_q = sr_ref[...]
        kt_ref[...] = k_ref[...].T
        acc_ref[...] = jnp.zeros_like(acc_ref)
        dv_total = jnp.zeros((1, 2 * HD), F32)
        for c in range(SEQ // chunk):
            at = pl.ds(c * chunk, chunk)
            k = k_ref[at, :]
            v = v_ref[at, :]
            same = sc_ref[at, :] == seg_q
            dks, dvs = [], []
            for h in range(2):
                s = jnp.where(same, nt(k, qm[h]), MASKED)
                p = jnp.exp(s - lse_ref[0, h : h + 1, :])
                ds = (p * (nt(v, gm[h]) - inner[h])).astype(BF)
                dvs.append(nn(p.astype(BF), g))
                dks.append(nn(ds, q))
                half = pl.ds(h * HD, HD)
                acc_ref[half, :] += nn(kt_ref[half, at], ds)
            dk_ref[at, :] = jnp.where(first, dks[0], dks[1]).astype(BF)
            dv = jnp.where(first, dvs[0], dvs[1]).astype(BF)
            dv_ref[at, :] = dv
            dv_total += jnp.sum(dv.astype(F32), 0, keepdims=True)
        dq = (acc_ref[...].T * SCALE).astype(BF)
        dq_ref[...] = dq
        sum_ref[0:1, :] = jnp.sum(dq.astype(F32), 0, keepdims=True)
        sum_ref[1:2, :] = dv_total

    spec = lambda off: pl.BlockSpec((SEQ, 2 * HD), lambda i: (0, i + off))
    full = lambda s: pl.BlockSpec(s, lambda i: (0,) * len(s))
    return pl.pallas_call(
        kernel,
        grid=(PAIRS,),
        in_specs=[spec(0), spec(PAIRS), spec(2 * PAIRS), spec(0), spec(0),
                  pl.BlockSpec((1, 8, SEQ), lambda i: (i, 0, 0)), full((SEQ, 1)), full((1, SEQ))],
        out_specs=[spec(0), spec(0), spec(0), pl.BlockSpec((8, 2 * HD), lambda i: (0, i))],
        out_shape=[jax.ShapeDtypeStruct((SEQ, D), BF)] * 3 + [jax.ShapeDtypeStruct((8, D), F32)],
        scratch_shapes=[pltpu.VMEM((2 * HD, SEQ), F32), pltpu.VMEM((2 * HD, SEQ), BF)],
        compiler_params=params(),
        name="attend_back",
    )(qkv, qkv, qkv, context, grad_context, lse, seg_col, seg_row)


def middle(me, context, x, g, vectors, up_bias, weight2, weight3):
    kind, refs2 = weight2
    _, refs3 = weight3
    count = 4 * refs2[0].shape[0] if kind == "pieces" else 1

    def kernel(me_ref, c_ref, x_ref, g_ref, vec_ref, ub_ref, *rest):
        w2, w3 = rest[: len(refs2)], rest[len(refs2) : len(refs2) + len(refs3)]
        (out_ref, act_ref, gpre_ref, n1_ref, gffn_ref, gattn_ref, gres_ref, gctx_ref,
         sum_ref, usum_ref, wo, wu, wd, slope, s_o, s_u, s_d) = rest[len(refs2) + len(refs3) :]
        step = pl.program_id(0)
        high, core = bits_of(me_ref)
        co = weight_copies(kind, w2, (0, D // 2), (0, D), wo, s_o, (high, core))
        cu = weight_copies(kind, w2, (D // 2, FF // 2), (D, FF), wu, s_u, (high, core))
        cd = weight_copies(kind, w3, (0, D // 2), (0, D), wd, s_d, (core, high))

        @pl.when(step == 0)
        def _():
            start_all(co)
            start_all(cu)
            start_all(cd)
            sum_ref[...] = jnp.zeros_like(sum_ref)
            usum_ref[...] = jnp.zeros_like(usum_ref)
            wait_all(co)

        out_bias, gain1, shift1 = vec_ref[0:1], vec_ref[1:2], vec_ref[2:3]
        down_bias, gain2, shift2 = vec_ref[3:4], vec_ref[4:5], vec_ref[5:6]
        attn = nn(c_ref[...], wo[...]) + out_bias
        xhat1, rstd1 = norm_rows(x_ref[...].astype(F32) + attn)
        normed1 = xhat1 * gain1 + shift1
        low1 = normed1.astype(BF)
        n1_ref[...] = low1

        @pl.when(step == 0)
        def _():
            wait_all(cu)
            wait_all(cd)

        ffn = jnp.zeros((ROWS, D), F32)
        for lo in range(0, FF, D):
            at = slice(lo, lo + D)
            pre = nn(low1, wu[:, at]) + ub_ref[:, at]
            act, sl = gelu_with_slope(pre)
            act = act.astype(BF)
            act_ref[:, at] = act
            slope[:, at] = sl
            ffn = ffn + nn(act, wd[at, :])
        xhat2, rstd2 = norm_rows(normed1 + (ffn + down_bias))
        out_ref[...] = (xhat2 * gain2 + shift2).astype(BF)
        gr = g_ref[...].astype(F32)
        res2 = norm_rows_back(gr * gain2, xhat2, rstd2)
        gffn = res2.astype(BF)
        gffn_ref[...] = gffn
        rs = lambda v: jnp.sum(v, 0, keepdims=True)
        sum_ref[0:1] += rs(gr * xhat2)
        sum_ref[1:2] += rs(gr)
        sum_ref[2:3] += rs(gffn.astype(F32))
        gn1 = res2
        for lo in range(0, FF, D):
            at = slice(lo, lo + D)
            gpre = (nt(gffn, wd[at, :]) * slope[:, at]).astype(BF)
            gpre_ref[:, at] = gpre
            usum_ref[0:1, at] += rs(gpre.astype(F32))
            gn1 = gn1 + nt(gpre, wu[:, at])
        sum_ref[3:4] += rs(gn1 * xhat1)
        sum_ref[4:5] += rs(gn1)
        res1 = norm_rows_back(gn1 * gain1, xhat1, rstd1)
        gres_ref[...] = res1
        gattn = res1.astype(BF)
        gattn_ref[...] = gattn
        sum_ref[5:6] += rs(gattn.astype(F32))
        gctx_ref[...] = nt(gattn, wo[...]).astype(BF)

    rows = x.shape[0]
    blk = lambda n: pl.BlockSpec((ROWS, n), lambda i, me: (i, 0))
    full = lambda s: pl.BlockSpec(s, lambda i, me: (0,) * len(s))
    sd = jax.ShapeDtypeStruct
    return pl.pallas_call(
        kernel,
        grid_spec=pltpu.PrefetchScalarGridSpec(
            num_scalar_prefetch=1,
            grid=(rows // ROWS,),
            in_specs=[blk(D), blk(D), blk(D), full((8, D)), full((1, FF))]
            + [ANY] * (len(refs2) + len(refs3)),
            out_specs=[blk(D), blk(FF), blk(FF), blk(D), blk(D), blk(D), blk(D), blk(D),
                       full((8, D)), full((8, FF))],
            scratch_shapes=[
                pltpu.VMEM((D, D), BF), pltpu.VMEM((D, FF), BF), pltpu.VMEM((FF, D), BF),
                pltpu.VMEM((ROWS, FF), F32),
                pltpu.SemaphoreType.DMA((count,)), pltpu.SemaphoreType.DMA((count,)),
                pltpu.SemaphoreType.DMA((count,)),
            ],
        ),
        out_shape=[sd((rows, D), BF), sd((rows, FF), BF), sd((rows, FF), BF), sd((rows, D), BF),
                   sd((rows, D), BF), sd((rows, D), BF), sd((rows, D), F32), sd((rows, D), BF),
                   sd((8, D), F32), sd((8, FF), F32)],
        compiler_params=params(),
        name="middle",
    )(me, context, x, g, vectors, up_bias, *refs2, *refs3)


def grad_down(me, act, grad_ffn, fsdp):
    per = FF // fsdp
    steps = 8
    width = FF // steps
    inner = width // per

    def kernel(me_ref, a_ref, g_ref, send_ref, keep_ref, acc_ref):
        _, core = bits_of(me_ref)
        acc_ref[...] = tn(a_ref[...], g_ref[...])
        n = per // 2
        for i in range(inner):
            take = lambda b: acc_ref[pl.ds(pl.multiple_of(i * per + n * b, n), n), :].astype(BF)
            send_ref[i] = take(1 - core)
            keep_ref[i] = take(core)

    rows = act.shape[0]
    out = jax.ShapeDtypeStruct((fsdp, per // 2, D), BF)
    ospec = pl.BlockSpec((inner, per // 2, D), lambda i, me: (i, 0, 0))
    return pl.pallas_call(
        kernel,
        grid_spec=pltpu.PrefetchScalarGridSpec(
            num_scalar_prefetch=1,
            grid=(steps,),
            in_specs=[pl.BlockSpec((rows, width), lambda i, me: (0, i)),
                      pl.BlockSpec((rows, D), lambda i, me: (0, 0))],
            out_specs=[ospec, ospec],
            scratch_shapes=[pltpu.VMEM((width, D), F32)],
        ),
        out_shape=[out, out],
        compiler_params=params(),
        name="grad_down",
    )(me, act, grad_ffn)


def halves_out(rows, width):
    specs = [pl.BlockSpec((rows, width), lambda i, me: (0, 0))] * 2
    shapes = [jax.ShapeDtypeStruct((rows, width), BF)] * 2
    return specs, shapes


def half_of(i, core):
    return jnp.where(i == 0, 1 - core, core)


def grad_up_out(me, low1, grad_pre, context, grad_attn):
    wu, wo = FF // 2, D // 2

    def kernel(me_ref, l_ref, p_ref, c_ref, a_ref, send_ref, keep_ref):
        def fill(o_ref):
            o_ref[:, :wo] = tn(c_ref[...], a_ref[...]).astype(BF)
            low = l_ref[...]
            for lo in range(0, wu, D):
                o_ref[:, wo + lo : wo + lo + D] = tn(low, p_ref[:, lo : lo + D]).astype(BF)

        pl.when(pl.program_id(0) == 0)(lambda: fill(send_ref))
        pl.when(pl.program_id(0) == 1)(lambda: fill(keep_ref))

    rows = low1.shape[0]
    half = lambda n: pl.BlockSpec(
        (rows, n), lambda i, me: (0, half_of(i, lax.bitwise_and(me[0], 1))))
    full = pl.BlockSpec((rows, D), lambda i, me: (0, 0))
    specs, shapes = halves_out(D, wu + wo)
    return pl.pallas_call(
        kernel,
        grid_spec=pltpu.PrefetchScalarGridSpec(
            num_scalar_prefetch=1, grid=(2,),
            in_specs=[full, half(wu), full, half(wo)], out_specs=specs),
        out_shape=shapes,
        compiler_params=params(),
        name="grad_up_out",
    )(me, low1, grad_pre, context, grad_attn)


def grad_qkv(me, x, dq, dk, dv):
    w = 3 * D // 2

    def kernel(me_ref, x_ref, q_ref, k_ref, v_ref, send_ref, keep_ref):
        _, core = bits_of(me_ref)

        def fill(o_ref, b):
            @pl.when(b == 0)
            def _():
                o_ref[:, :D] = tn(x_ref[...], q_ref[...]).astype(BF)
                o_ref[:, D:] = tn(x_ref[...], k_ref[:, : D // 2]).astype(BF)

            @pl.when(b == 1)
            def _():
                o_ref[:, : D // 2] = tn(x_ref[...], k_ref[:, D // 2 :]).astype(BF)
                o_ref[:, D // 2 :] = tn(x_ref[...], v_ref[...]).astype(BF)

        pl.when(pl.program_id(0) == 0)(lambda: fill(send_ref, 1 - core))
        pl.when(pl.program_id(0) == 1)(lambda: fill(keep_ref, core))

    rows = x.shape[0]
    full = pl.BlockSpec((rows, D), lambda i, me: (0, 0))
    specs, shapes = halves_out(D, w)
    return pl.pallas_call(
        kernel,
        grid_spec=pltpu.PrefetchScalarGridSpec(
            num_scalar_prefetch=1, grid=(2,), in_specs=[full] * 4, out_specs=specs),
        out_shape=shapes,
        compiler_params=params(),
        name="grad_qkv",
    )(me, x, dq, dk, dv)


def grad_in(me, dq, dk, dv, res1, weight):
    kind, refs = weight
    n = 3 * D
    count = 4 * refs[0].shape[0] if kind == "pieces" else 1

    def kernel(me_ref, q_ref, k_ref, v_ref, r_ref, *rest):
        w_refs, (o_ref, w_ref, sems) = rest[:-3], rest[-3:]

        @pl.when(pl.program_id(0) == 0)
        def _():
            high, core = bits_of(me_ref)
            copies = weight_copies(kind, w_refs, (0, n // 2), (0, n), w_ref, sems, (high, core))
            start_all(copies)
            wait_all(copies)

        total = r_ref[...] + nt(q_ref[...], w_ref[:, :D])
        total = total + nt(k_ref[...], w_ref[:, D : 2 * D])
        total = total + nt(v_ref[...], w_ref[:, 2 * D :])
        o_ref[...] = total.astype(BF)

    rows = dq.shape[0]
    blk = pl.BlockSpec((ROWS, D), lambda i, me: (i, 0))
    return pl.pallas_call(
        kernel,
        grid_spec=pltpu.PrefetchScalarGridSpec(
            num_scalar_prefetch=1, grid=(rows // ROWS,),
            in_specs=[blk] * 4 + [ANY] * len(refs), out_specs=blk,
            scratch_shapes=[pltpu.VMEM((D, n), BF), pltpu.SemaphoreType.DMA((count,))]),
        out_shape=jax.ShapeDtypeStruct((rows, D), BF),
        compiler_params=params(),
        name="grad_in",
    )(me, dq, dk, dv, res1, *refs)


def local(hidden_in, doc_starts, w_qkv, query_bias, value_bias, w_out, out_bias, norm1_gain,
          norm1_bias, w_up, up_bias, w_down, down_bias, norm2_gain, norm2_bias, cotangent):
    fsdp, sp = lax.axis_size("fsdp"), lax.axis_size("sp")
    seqs, span, _ = hidden_in.shape
    assert sp == 4 and seqs == sp and span * sp == SEQ
    me = lax.axis_index("sp").astype(jnp.int32)
    core, high = me & 1, me >> 1
    me1 = me.reshape(1)
    rows_d, rows_f = D // fsdp, FF // fsdp
    split = rows_d % 32 == 0 and rows_f % 32 == 0

    def partner(v, bit):
        return lax.ppermute(v, "sp", [(i, i ^ bit) for i in range(sp)])

    def spread(v):
        return lax.all_to_all(jnp.broadcast_to(v[None], (fsdp,) + v.shape), "fsdp", 0, 0, tiled=True)

    def quarter(w, row_bit, col_bit):
        r, c = w.shape[0] // 2, w.shape[1] // 2
        return lax.dynamic_slice(w, (row_bit * r, col_bit * c), (r, c))

    x = lax.all_to_all(hidden_in, "sp", 0, 0, tiled=True).reshape(SEQ, D)

    small = jnp.concatenate([out_bias, norm1_gain, norm1_bias, down_bias, norm2_gain, norm2_bias,
                             query_bias, value_bias, up_bias])
    if split:
        q1 = quarter(w_qkv, high, core)
        pad = jnp.zeros((16, q1.shape[1]), BF).at[0].set(small)
        a = spread(jnp.concatenate([q1, pad], 0))
        every = a[:, q1.shape[0]]
        a = a[:, : q1.shape[0]]
    else:
        every = lax.all_gather(small, "fsdp", axis=0)

    def pieces(a):
        b = partner(a, 2)
        return ("pieces", (a, partner(a, 1), b, partner(b, 1)))

    if split:
        weight1 = pieces(a)
        a2 = spread(jnp.concatenate([quarter(w_out, high, core), quarter(w_up, high, core)], 1))
        weight2 = pieces(a2)
        a3 = spread(quarter(w_down, core, high))
        b3 = partner(a3, 2)
        weight3 = ("pieces", (a3, b3, partner(a3, 1), partner(b3, 1)))
    else:
        gather = lambda w: lax.all_gather(w, "fsdp", axis=0, tiled=True)
        weight1 = ("whole", (gather(w_qkv),))
        weight2 = ("whole", (gather(jnp.concatenate([w_out, w_up], 1)),))
        weight3 = ("whole", (gather(w_down),))
    g = lax.all_to_all(cotangent, "sp", 0, 0, tiled=True).reshape(SEQ, D)

    every = every.astype(F32)
    table = every[:, : 8 * rows_d].reshape(fsdp, 8, rows_d).transpose(1, 0, 2).reshape(8, D)
    full_up_bias = every[:, 8 * rows_d :].reshape(1, FF)
    bias_row = jnp.concatenate([table[6:7], jnp.zeros((1, D), F32), table[7:8]], 1)

    starts = lax.dynamic_slice(doc_starts, (me, 0), (1, doc_starts.shape[1]))
    seg = jnp.sum((jnp.arange(SEQ, dtype=jnp.int32)[:, None] >= starts).astype(jnp.int32), -1)
    seg_col, seg_row = seg[:, None], seg[None, :]

    qkv = project(me1, x, weight1, bias_row)
    context, lse = attend(qkv, seg_col, seg_row)
    (out, act, gpre, low1, gffn, gattn, res1, gctx, sums, up_sums) = middle(
        me1, context, x, g, table, full_up_bias, weight2, weight3)
    layer_out = lax.all_to_all(out.reshape(seqs, span, D), "sp", 0, 0, tiled=True)

    def finish(v, row_first):
        parts = lax.all_to_all(v, "fsdp", 0, 0, tiled=True)
        mine = jnp.sum(parts.astype(F32), 0).astype(BF)
        return mine

    def join(mine, other, bit, axis):
        return jnp.where(bit == 0, jnp.concatenate([mine, other], axis),
                         jnp.concatenate([other, mine], axis))

    if split:
        def reduce_rows(send, keep, extra=None):
            half = (keep.astype(F32) + partner(send, 1).astype(F32)).astype(BF)
            width = half.shape[1]
            cut = half[:D].reshape(fsdp, 2, rows_d // 2, width)
            take = lambda b: lax.dynamic_index_in_dim(cut, b, 1, False)
            mine, theirs = take(high), take(1 - high)
            if extra is not None:
                e = half[D : D + fsdp].reshape(fsdp, 1, width)
                mine = jnp.concatenate([mine, e], 1)
                theirs = jnp.concatenate([theirs, e], 1)
            whole = (mine.astype(F32) + partner(theirs, 2).astype(F32)).astype(BF)
            total = finish(whole, True)
            tail = total[rows_d // 2 :]
            total = total[: rows_d // 2]
            total = join(total, partner(total, 2), high, 0)
            total = join(total, partner(total, 1), core, 1).astype(F32)
            return (total, tail.astype(F32)) if extra is not None else total

        def reduce_down(send, keep):
            half = (keep.astype(F32) + partner(send, 1).astype(F32)).astype(BF)
            take = lambda b: lax.dynamic_slice(half, (0, 0, b * (D // 2)), (fsdp, rows_f // 2, D // 2))
            whole = (take(high).astype(F32) + partner(take(1 - high), 2).astype(F32)).astype(BF)
            total = finish(whole, False)
            total = join(total, partner(total, 2), high, 1)
            return join(total, partner(total, 1), core, 0).astype(F32)
    else:
        def scatter(v):
            part = lax.psum_scatter(v, "fsdp", scatter_dimension=0, tiled=True)
            return lax.psum(part, "sp").astype(F32)

        def reduce_rows(send, keep, extra=None):
            total = scatter(join(keep, send, core, 1)[:D].astype(F32))
            if extra is None:
                return total
            e = lax.psum_scatter(extra.astype(F32), "fsdp", scatter_dimension=0, tiled=True)
            return total, lax.psum(e, "sp").astype(F32)

        def reduce_down(send, keep):
            return scatter(join(keep, send, core, 1).reshape(FF, D).astype(F32))

    down = reduce_down(*grad_down(me1, act, gffn, fsdp))
    wide = reduce_rows(*grad_up_out(me1, low1, gpre, context, gattn))
    dq, dk, dv, bias_sums = attend_back(qkv, context, gctx, lse, seg_col, seg_row)
    send, keep = grad_qkv(me1, x, dq, dk, dv)

    by_dest = jnp.concatenate([sums[:6], bias_sums[:2]], 0).reshape(8, fsdp, rows_d)
    by_dest = by_dest.transpose(1, 0, 2).reshape(fsdp, 8 * rows_d)
    extra = jnp.concatenate([by_dest, up_sums[0].reshape(fsdp, rows_f)], 1).astype(BF)
    if split:
        send = jnp.concatenate([send, extra], 0)
        keep = jnp.concatenate([keep, extra], 0)
    qkv_grad, tail = reduce_rows(send, keep, extra)
    dx = grad_in(me1, dq, dk, dv, res1, weight1)
    grad_input = lax.all_to_all(dx.reshape(seqs, span, D), "sp", 0, 0, tiled=True)

    tail = tail.reshape(-1)
    vec = [tail[i * rows_d : (i + 1) * rows_d] for i in range(8)]
    g2, b2, db, g1, b1, ob, qb, vb = vec
    ub = tail[8 * rows_d :]
    if split:
        w1, w2 = D // 2, FF // 2
        grad_out = jnp.concatenate([wide[:, :w1], wide[:, w1 + w2 : 2 * w1 + w2]], 1)
        grad_up = jnp.concatenate([wide[:, w1 : w1 + w2], wide[:, 2 * w1 + w2 :]], 1)
    else:
        w1, w2 = D // 2, FF // 2
        grad_out = jnp.concatenate([wide[:, :w1], wide[:, w1 + w2 : 2 * w1 + w2]], 1)
        grad_up = jnp.concatenate([wide[:, w1 : w1 + w2], wide[:, 2 * w1 + w2 :]], 1)
    return (layer_out, grad_input, qkv_grad, qb, vb, grad_out, ob, g1, b1, grad_up, ub, down, db,
            g2, b2)


def solution(mesh):
    tok = P("fsdp", "sp", None)
    mat, vec = P("fsdp", None), P("fsdp")
    in_specs = (tok, mat, mat, vec, vec, mat, vec, vec, vec, mat, vec, mat, vec, vec, vec, tok)
    out_specs = (tok, tok, mat, vec, vec, mat, vec, vec, vec, mat, vec, mat, vec, vec, vec)
    return jax.shard_map(local, mesh=mesh, in_specs=in_specs, out_specs=out_specs, check_vma=False)
```

```python
import jax
import jax.numpy as jnp
from jax import lax
from jax.experimental import pallas as pl
from jax.experimental.pallas import tpu as pltpu
from jax.sharding import PartitionSpec as P


D = 768
H = 12
HD = 64
FF = 3072
SEQ = 1024
PAIRS = H // 2
EPS = 1e-05
MASKED = -1000000000.0
SCALE = HD ** (-0.5)
BF = jnp.bfloat16
F32 = jnp.float32
ROWS = 256
MIB = 1 << 20


ERFC = (
    0.2820844758103095,
    0.28240952292464144,
    0.24285408258103366,
    0.20367679547693512,
    -0.028968306758876145,
    0.2814702272328375,
    -0.49017537256556365,
    0.28601194065835034,
    -0.059363409284156475,
)


def nn(a, b):
    return lax.dot_general(a, b, (((1,), (0,)), ((), ())), preferred_element_type=F32)


def nt(a, b):
    return lax.dot_general(a, b, (((1,), (1,)), ((), ())), preferred_element_type=F32)


def tn(a, b):
    return lax.dot_general(a, b, (((0,), (0,)), ((), ())), preferred_element_type=F32)


def gelu_with_slope(x):
    z = jnp.abs(x) * 0.7071067811865476
    t = 1.0 / (1.0 + 0.5 * z)
    e = jnp.exp(-0.5 * (x * x))
    poly = jnp.full_like(t, 0.5 * ERFC[-1])
    for c in ERFC[-2::-1]:
        poly = poly * t + 0.5 * c
    tail = poly * t * e
    cdf = jnp.where(x >= 0, 1.0 - tail, tail)
    return x * cdf, cdf + x * (e * 0.3989422804014327)


def norm_rows(v):
    c = v - jnp.mean(v, -1, keepdims=True)
    r = lax.rsqrt(jnp.mean(c * c, -1, keepdims=True) + EPS)
    return c * r, r


def norm_rows_back(a, xhat, rstd):
    return rstd * (a - jnp.mean(a, -1, keepdims=True) - xhat * jnp.mean(a * xhat, -1, keepdims=True))


def piece_copies(pieces, by_rows, cols, dst, sems, core, x_bit):
    copies = []
    lo, nc = cols
    for rc, ref in enumerate(pieces):
        _, count, nr, _ = ref.shape
        nr -= nr % (D // 8 // 2) if not by_rows else 0
        row0 = nr * lax.bitwise_xor(core, rc) if by_rows else 0
        col0 = 0 if by_rows else nc * lax.bitwise_xor(core, rc)
        stride = nr * (2 if by_rows else 1)
        for rx in range(2):
            for z in range(count):
                row = row0 + stride * (2 * z + lax.bitwise_xor(x_bit, rx))
                copies.append(
                    pltpu.make_async_copy(
                        ref.at[rx, z, pl.ds(0, nr), pl.ds(lo, nc)],
                        dst.at[
                            pl.ds(pl.multiple_of(row, nr), nr),
                            pl.ds(0 if by_rows else pl.multiple_of(col0, nc), nc),
                        ],
                        sems.at[(rc * 2 + rx) * count + z],
                    )
                )
    return copies


def whole_copies(ref, cols, dst, sems):
    lo, nc = cols
    return [pltpu.make_async_copy(ref.at[:, pl.ds(lo, nc)], dst, sems.at[0])]


def weight_copies(kind, refs, cols, full_cols, dst, sems, bits):
    if kind == "whole":
        return whole_copies(refs[0], full_cols, dst, sems)
    return piece_copies(refs, kind == "rows", full_cols if kind == "rows" else cols, dst, sems, *bits)


def copy_count(weight):
    kind, refs = weight
    return 1 if kind == "whole" else 4 * refs[0].shape[1]


def put_block(refs, step, value):
    for r, ref in enumerate(refs):
        @pl.when(step == r)
        def _():
            ref[...] = value


def start_all(copies):
    for c in copies:
        c.start()


def wait_all(copies):
    for c in copies:
        c.wait()


ANY = pl.BlockSpec(memory_space=pl.ANY)


def cost(us):
    return pl.CostEstimate(flops=int(us * 1e9), bytes_accessed=1 << 20, transcendentals=0)


def params(vmem=58):
    return pltpu.CompilerParams(
        dimension_semantics=("arbitrary",), vmem_limit_bytes=vmem * MIB
    )


def bits_of(me_ref):
    return lax.bitwise_and(me_ref[0], 1), me_ref[1]


def pack(me, w, vectors, copies):
    rows, width = w.shape[0], w.shape[1] // 2

    def kernel(me_ref, w_ref, *rest):
        v_refs, o_ref = rest[:-1], rest[-1]
        for z in range(copies):
            o_ref[z, :rows, :] = w_ref[...]
            o_ref[z, rows:, :] = jnp.zeros((16, width), BF)
        for i, v in enumerate(v_refs):
            for z in range(copies):
                o_ref[z, rows + i : rows + i + 1, : v.shape[0]] = v[...].reshape(1, -1)

    one = lambda v: pl.BlockSpec(v.shape, lambda i, me: (0,))
    return pl.pallas_call(
        kernel,
        grid_spec=pltpu.PrefetchScalarGridSpec(
            num_scalar_prefetch=1,
            grid=(1,),
            in_specs=[pl.BlockSpec((rows, width), lambda i, me: (0, lax.bitwise_and(me[0], 1)))]
            + [one(v) for v in vectors],
            out_specs=pl.BlockSpec((copies, rows + 16, width), lambda i, me: (0, 0, 0)),
        ),
        out_shape=jax.ShapeDtypeStruct((copies, rows + 16, width), BF),
        compiler_params=params(),
        cost_estimate=cost(2),
        name="pack",
    )(me, w, *vectors)


def deal(me, v):
    def kernel(me_ref, v_ref, *rest):
        o_refs, sems = rest[:-1], rest[-1]
        copies = [pltpu.make_async_copy(v_ref.at[lax.bitwise_xor(me_ref[0], r)], o, sems.at[r])
                  for r, o in enumerate(o_refs)]
        start_all(copies)
        wait_all(copies)

    n = v.shape[0]
    return pl.pallas_call(
        kernel,
        in_specs=[pl.BlockSpec(memory_space=pltpu.SMEM), ANY],
        out_specs=[ANY] * n,
        out_shape=[jax.ShapeDtypeStruct(v.shape[1:], v.dtype)] * n,
        scratch_shapes=[pltpu.SemaphoreType.DMA((n,))],
        cost_estimate=cost(2),
        name="deal",
    )(me, v)


def place(me, parts):
    def kernel(me_ref, *rest):
        p_refs, (o_ref, sems) = rest[:-2], rest[-2:]
        copies = [pltpu.make_async_copy(p, o_ref.at[lax.bitwise_xor(me_ref[0], r)], sems.at[r])
                  for r, p in enumerate(p_refs)]
        start_all(copies)
        wait_all(copies)

    n = len(parts)
    return pl.pallas_call(
        kernel,
        in_specs=[pl.BlockSpec(memory_space=pltpu.SMEM)] + [ANY] * n,
        out_specs=ANY,
        out_shape=jax.ShapeDtypeStruct((n,) + parts[0].shape, parts[0].dtype),
        scratch_shapes=[pltpu.SemaphoreType.DMA((n,))],
        cost_estimate=cost(2),
        name="place",
    )(me, *parts)


def project(me, x, weight, bias_row):
    kind, refs = weight
    n = 3 * D
    count = copy_count(weight)

    def kernel(me_ref, x_ref, b_ref, *rest):
        w_refs, (o_ref, w_ref, sems) = rest[:-3], rest[-3:]

        @pl.when(pl.program_id(0) == 0)
        def _():
            copies = weight_copies(kind, w_refs, (0, n // 2), (0, n), w_ref, sems, bits_of(me_ref))
            start_all(copies)
            wait_all(copies)

        xv = x_ref[...]
        for lo in range(0, n, D):
            o_ref[:, lo : lo + D] = (
                nn(xv, w_ref[:, lo : lo + D]) + b_ref[:, lo : lo + D]
            ).astype(BF)

    rows = x.shape[0]
    return pl.pallas_call(
        kernel,
        grid_spec=pltpu.PrefetchScalarGridSpec(
            num_scalar_prefetch=1,
            grid=(rows // ROWS,),
            in_specs=[
                pl.BlockSpec((ROWS, D), lambda i, me: (i, 0)),
                pl.BlockSpec((1, n), lambda i, me: (0, 0)),
            ]
            + [ANY] * len(refs),
            out_specs=pl.BlockSpec((ROWS, n), lambda i, me: (i, 0)),
            scratch_shapes=[pltpu.VMEM((D, n), BF), pltpu.SemaphoreType.DMA((count,))],
        ),
        out_shape=jax.ShapeDtypeStruct((rows, n), BF),
        compiler_params=params(),
        cost_estimate=cost(9),
        name="project",
    )(me, x, bias_row, *refs)


def attend(qkv, seg_col, seg_row, first, count, before):
    chunk = 256

    def kernel(q_ref, k_ref, v_ref, sc_ref, sr_ref, *rest):
        o_ref, lse_ref = rest[-2:]
        lane = lax.broadcasted_iota(jnp.int32, (1, 2 * HD), 1)
        k = k_ref[...]
        vt = v_ref[...].T
        seg_k = sc_ref[...]
        for c in range(SEQ // chunk):
            at = pl.ds(c * chunk, chunk)
            q = q_ref[at, :] * jnp.asarray(SCALE, BF)
            same = seg_k == sr_ref[:, at]
            outs = []
            for h in range(2):
                mine = (lane < HD) if h == 0 else (lane >= HD)
                s = nt(k, jnp.where(mine, q, jnp.zeros_like(q)))
                s = jnp.where(same, s, MASKED)
                m = jnp.max(s, 0, keepdims=True)
                p = jnp.exp(s - m)
                l = jnp.sum(p, 0, keepdims=True)
                lse_ref[0, h : h + 1, at] = m + jnp.log(l)
                o = nn(vt, p.astype(BF))
                outs.append(o[h * HD : (h + 1) * HD] * (1.0 / l))
            o_ref[at, :] = jnp.concatenate(outs, 0).T.astype(BF)

    spec = lambda off: pl.BlockSpec((SEQ, 2 * HD), lambda i: (0, i + off + first))
    full = lambda s: pl.BlockSpec(s, lambda i: (0,) * len(s))
    return pl.pallas_call(
        kernel,
        grid=(count,),
        in_specs=[spec(0), spec(PAIRS), spec(2 * PAIRS), full((SEQ, 1)), full((1, SEQ))]
        + [ANY] * len(before),
        out_specs=[spec(0), pl.BlockSpec((1, 8, SEQ), lambda i: (i + first, 0, 0))],
        input_output_aliases={5 + i: i for i in range(len(before))},
        out_shape=[
            jax.ShapeDtypeStruct((SEQ, D), BF),
            jax.ShapeDtypeStruct((PAIRS, 8, SEQ), F32),
        ],
        compiler_params=params(),
        cost_estimate=cost(6 * count),
        name="attend",
    )(qkv, qkv, qkv, seg_col, seg_row, *before)


def attend_back(qkv, context, grad_context, lse, seg_col, seg_row, start, count, before):
    chunk = 256

    def kernel(q_ref, k_ref, v_ref, o_ref, g_ref, lse_ref, sc_ref, sr_ref, *rest):
        dq_ref, dk_ref, dv_ref, sum_ref, acc_ref, kt_ref = rest[-6:]
        lane = lax.broadcasted_iota(jnp.int32, (1, 2 * HD), 1)
        first = lane < HD
        q = q_ref[...] * jnp.asarray(SCALE, BF)
        g = g_ref[...]
        zero = jnp.zeros_like(q)
        prod = (g.astype(F32) * o_ref[...].astype(F32)).T
        inner = [jnp.sum(prod[h * HD : (h + 1) * HD], 0, keepdims=True) for h in range(2)]
        qm = [jnp.where(first, q, zero), jnp.where(first, zero, q)]
        gm = [jnp.where(first, g, zero), jnp.where(first, zero, g)]
        seg_q = sr_ref[...]
        kt_ref[...] = k_ref[...].T
        acc_ref[...] = jnp.zeros_like(acc_ref)
        dv_total = jnp.zeros((1, 2 * HD), F32)
        for c in range(SEQ // chunk):
            at = pl.ds(c * chunk, chunk)
            k = k_ref[at, :]
            v = v_ref[at, :]
            same = sc_ref[at, :] == seg_q
            dks, dvs = [], []
            for h in range(2):
                s = jnp.where(same, nt(k, qm[h]), MASKED)
                p = jnp.exp(s - lse_ref[0, h : h + 1, :])
                ds = (p * (nt(v, gm[h]) - inner[h])).astype(BF)
                dvs.append(nn(p.astype(BF), g))
                dks.append(nn(ds, q))
                half = pl.ds(h * HD, HD)
                acc_ref[half, :] += nn(kt_ref[half, at], ds)
            dk_ref[at, :] = jnp.where(first, dks[0], dks[1]).astype(BF)
            dv = jnp.where(first, dvs[0], dvs[1]).astype(BF)
            dv_ref[at, :] = dv
            dv_total += jnp.sum(dv.astype(F32), 0, keepdims=True)
        dq = (acc_ref[...].T * SCALE).astype(BF)
        dq_ref[...] = dq
        sum_ref[0:1, :] = jnp.sum(dq.astype(F32), 0, keepdims=True)
        sum_ref[1:2, :] = dv_total

    spec = lambda off: pl.BlockSpec((SEQ, 2 * HD), lambda i: (0, i + off + start))
    full = lambda s: pl.BlockSpec(s, lambda i: (0,) * len(s))
    return pl.pallas_call(
        kernel,
        grid=(count,),
        in_specs=[spec(0), spec(PAIRS), spec(2 * PAIRS), spec(0), spec(0),
                  pl.BlockSpec((1, 8, SEQ), lambda i: (i + start, 0, 0)), full((SEQ, 1)),
                  full((1, SEQ))] + [ANY] * len(before),
        out_specs=[spec(0), spec(0), spec(0), pl.BlockSpec((8, 2 * HD), lambda i: (0, i + start))],
        input_output_aliases={8 + i: i for i in range(len(before))},
        out_shape=[jax.ShapeDtypeStruct((SEQ, D), BF)] * 3 + [jax.ShapeDtypeStruct((8, D), F32)],
        scratch_shapes=[pltpu.VMEM((2 * HD, SEQ), F32), pltpu.VMEM((2 * HD, SEQ), BF)],
        compiler_params=params(),
        cost_estimate=cost(6 * count),
        name="attend_back",
    )(qkv, qkv, qkv, context, grad_context, lse, seg_col, seg_row, *before)


def middle(me, context, x, g, vectors, up_bias, weight2, weight3):
    kind2, refs2 = weight2
    kind3, refs3 = weight3
    count = copy_count(weight2)
    blocks = x.shape[0] // ROWS

    def kernel(me_ref, c_ref, x_ref, g_ref, vec_ref, ub_ref, *rest):
        w2, w3 = rest[: len(refs2)], rest[len(refs2) : len(refs2) + len(refs3)]
        o_refs = rest[len(refs2) + len(refs3) :][:blocks]
        (act_ref, gpre_ref, n1_ref, gffn_ref, gattn_ref, gres_ref, gctx_ref,
         sum_ref, usum_ref, wo, wu, wd, slope, s_o, s_u, s_d) = rest[len(refs2) + len(refs3) + blocks :]
        step = pl.program_id(0)
        bits = bits_of(me_ref)
        co = weight_copies(kind2, w2, (0, D // 2), (0, D), wo, s_o, bits)
        cu = weight_copies(kind2, w2, (D // 2, FF // 2), (D, FF), wu, s_u, bits)
        cd = weight_copies(kind3, w3, None, (0, D), wd, s_d, bits)

        @pl.when(step == 0)
        def _():
            start_all(co)
            start_all(cu)
            start_all(cd)
            sum_ref[...] = jnp.zeros_like(sum_ref)
            usum_ref[...] = jnp.zeros_like(usum_ref)
            wait_all(co)

        out_bias, gain1, shift1 = vec_ref[0:1], vec_ref[1:2], vec_ref[2:3]
        down_bias, gain2, shift2 = vec_ref[3:4], vec_ref[4:5], vec_ref[5:6]
        attn = nn(c_ref[...], wo[...]) + out_bias
        xhat1, rstd1 = norm_rows(x_ref[...].astype(F32) + attn)
        normed1 = xhat1 * gain1 + shift1
        low1 = normed1.astype(BF)
        n1_ref[...] = low1

        @pl.when(step == 0)
        def _():
            wait_all(cu)
            wait_all(cd)

        ffn = jnp.zeros((ROWS, D), F32)
        for lo in range(0, FF, D):
            at = slice(lo, lo + D)
            pre = nn(low1, wu[:, at]) + ub_ref[:, at]
            act, sl = gelu_with_slope(pre)
            act = act.astype(BF)
            act_ref[:, at] = act
            slope[:, at] = sl
            ffn = ffn + nn(act, wd[at, :])
        xhat2, rstd2 = norm_rows(normed1 + (ffn + down_bias))
        out = (xhat2 * gain2 + shift2).astype(BF)
        put_block(o_refs, step, out)
        gr = g_ref[...].astype(F32)
        res2 = norm_rows_back(gr * gain2, xhat2, rstd2)
        gffn = res2.astype(BF)
        gffn_ref[...] = gffn
        rs = lambda v: jnp.sum(v, 0, keepdims=True)
        sum_ref[0:1] += rs(gr * xhat2)
        sum_ref[1:2] += rs(gr)
        sum_ref[2:3] += rs(gffn.astype(F32))
        gn1 = res2
        for lo in range(0, FF, D):
            at = slice(lo, lo + D)
            gpre = (nt(gffn, wd[at, :]) * slope[:, at]).astype(BF)
            gpre_ref[:, at] = gpre
            usum_ref[0:1, at] += rs(gpre.astype(F32))
            gn1 = gn1 + nt(gpre, wu[:, at])
        sum_ref[3:4] += rs(gn1 * xhat1)
        sum_ref[4:5] += rs(gn1)
        res1 = norm_rows_back(gn1 * gain1, xhat1, rstd1)
        gres_ref[...] = res1
        gattn = res1.astype(BF)
        gattn_ref[...] = gattn
        sum_ref[5:6] += rs(gattn.astype(F32))
        gctx_ref[...] = nt(gattn, wo[...]).astype(BF)

    rows = x.shape[0]
    blk = lambda n: pl.BlockSpec((ROWS, n), lambda i, me: (i, 0))
    full = lambda s: pl.BlockSpec(s, lambda i, me: (0,) * len(s))
    sd = jax.ShapeDtypeStruct
    return pl.pallas_call(
        kernel,
        grid_spec=pltpu.PrefetchScalarGridSpec(
            num_scalar_prefetch=1,
            grid=(rows // ROWS,),
            in_specs=[blk(D), blk(D), blk(D), full((8, D)), full((1, FF))]
            + [ANY] * (len(refs2) + len(refs3)),
            out_specs=[full((ROWS, D))] * blocks + [blk(FF), blk(FF), blk(D), blk(D), blk(D), blk(D), blk(D),
                       full((8, D)), full((8, FF))],
            scratch_shapes=[
                pltpu.VMEM((D, D), BF), pltpu.VMEM((D, FF), BF), pltpu.VMEM((FF, D), BF),
                pltpu.VMEM((ROWS, FF), F32),
                pltpu.SemaphoreType.DMA((count,)), pltpu.SemaphoreType.DMA((count,)),
                pltpu.SemaphoreType.DMA((count,)),
            ],
        ),
        out_shape=[sd((ROWS, D), BF)] * blocks + [sd((rows, FF), BF), sd((rows, FF), BF), sd((rows, D), BF),
                   sd((rows, D), BF), sd((rows, D), BF), sd((rows, D), F32), sd((rows, D), BF),
                   sd((8, D), F32), sd((8, FF), F32)],
        compiler_params=params(),
        cost_estimate=cost(48),
        name="middle",
    )(me, context, x, g, vectors, up_bias, *refs2, *refs3)


def grad_down(me, act, grad_ffn, fsdp):
    per = FF // fsdp
    steps = 8
    width = FF // steps
    inner = width // per

    def kernel(me_ref, a_ref, g_ref, send_ref, keep_ref, acc_ref):
        core, _ = bits_of(me_ref)
        acc_ref[...] = tn(a_ref[...], g_ref[...])
        n = per // 2
        for i in range(inner):
            take = lambda b: acc_ref[pl.ds(pl.multiple_of(i * per + n * b, n), n), :].astype(BF)
            send_ref[i] = take(1 - core)
            keep_ref[i] = take(core)

    rows = act.shape[0]
    out = jax.ShapeDtypeStruct((fsdp, per // 2, D), BF)
    ospec = pl.BlockSpec((inner, per // 2, D), lambda i, me: (i, 0, 0))
    return pl.pallas_call(
        kernel,
        grid_spec=pltpu.PrefetchScalarGridSpec(
            num_scalar_prefetch=1,
            grid=(steps,),
            in_specs=[pl.BlockSpec((rows, width), lambda i, me: (0, i)),
                      pl.BlockSpec((rows, D), lambda i, me: (0, 0))],
            out_specs=[ospec, ospec],
            scratch_shapes=[pltpu.VMEM((width, D), F32)],
        ),
        out_shape=[out, out],
        compiler_params=params(),
        cost_estimate=cost(12),
        name="grad_down",
    )(me, act, grad_ffn)


def halves_out(rows, width):
    specs = [pl.BlockSpec((rows, width), lambda i, me: (0, 0))] * 2
    shapes = [jax.ShapeDtypeStruct((rows, width), BF)] * 2
    return specs, shapes


def half_of(i, core):
    return jnp.where(i == 0, 1 - core, core)


def grad_up_out(me, low1, grad_pre, context, grad_attn):
    wu, wo = FF // 2, D // 2

    def kernel(me_ref, l_ref, p_ref, c_ref, a_ref, send_ref, keep_ref):
        def fill(o_ref):
            o_ref[:, :wo] = tn(c_ref[...], a_ref[...]).astype(BF)
            low = l_ref[...]
            for lo in range(0, wu, D):
                o_ref[:, wo + lo : wo + lo + D] = tn(low, p_ref[:, lo : lo + D]).astype(BF)

        pl.when(pl.program_id(0) == 0)(lambda: fill(send_ref))
        pl.when(pl.program_id(0) == 1)(lambda: fill(keep_ref))

    rows = low1.shape[0]
    half = lambda n: pl.BlockSpec(
        (rows, n), lambda i, me: (0, half_of(i, lax.bitwise_and(me[0], 1))))
    full = pl.BlockSpec((rows, D), lambda i, me: (0, 0))
    specs, shapes = halves_out(D, wu + wo)
    return pl.pallas_call(
        kernel,
        grid_spec=pltpu.PrefetchScalarGridSpec(
            num_scalar_prefetch=1, grid=(2,),
            in_specs=[full, half(wu), full, half(wo)], out_specs=specs),
        out_shape=shapes,
        compiler_params=params(),
        cost_estimate=cost(12),
        name="grad_up_out",
    )(me, low1, grad_pre, context, grad_attn)


def grad_qkv(me, x, dq, dk, dv, sums, up_sums, bias_sums, fsdp):
    w = 3 * D // 2
    per, per_up = D // fsdp, FF // fsdp
    tall = per + 16

    def kernel(me_ref, x_ref, q_ref, k_ref, v_ref, s_ref, u_ref, b_ref, send_ref, keep_ref):
        core, _ = bits_of(me_ref)

        def put(o_ref, lo, val):
            val = val.astype(BF)
            for d in range(fsdp):
                o_ref[d, :per, lo : lo + val.shape[1]] = val[d * per : (d + 1) * per]

        def fill(o_ref, b):
            @pl.when(b == 0)
            def _():
                put(o_ref, 0, tn(x_ref[...], q_ref[...]))
                put(o_ref, D, tn(x_ref[...], k_ref[:, : D // 2]))

            @pl.when(b == 1)
            def _():
                put(o_ref, 0, tn(x_ref[...], k_ref[:, D // 2 :]))
                put(o_ref, D // 2, tn(x_ref[...], v_ref[...]))

            rows = jnp.concatenate([s_ref[0:6], b_ref[0:2]], 0)
            for d in range(fsdp):
                o_ref[d, per:, :] = jnp.zeros((16, w), BF)
                o_ref[d, per : per + 8, :per] = rows[:, d * per : (d + 1) * per].astype(BF)
                o_ref[d, per + 8 : per + 9, :per_up] = u_ref[0:1, d * per_up : (d + 1) * per_up].astype(BF)

        pl.when(pl.program_id(0) == 0)(lambda: fill(send_ref, 1 - core))
        pl.when(pl.program_id(0) == 1)(lambda: fill(keep_ref, core))

    rows = x.shape[0]
    full = lambda s: pl.BlockSpec(s, lambda i, me: (0, 0))
    return pl.pallas_call(
        kernel,
        grid_spec=pltpu.PrefetchScalarGridSpec(
            num_scalar_prefetch=1, grid=(2,),
            in_specs=[full((rows, D))] * 4 + [full((8, D)), full((8, FF)), full((8, D))],
            out_specs=[pl.BlockSpec((fsdp, tall, w), lambda i, me: (0, 0, 0))] * 2),
        out_shape=[jax.ShapeDtypeStruct((fsdp, tall, w), BF)] * 2,
        compiler_params=params(),
        cost_estimate=cost(9),
        name="grad_qkv",
    )(me, x, dq, dk, dv, sums, up_sums, bias_sums)


def grad_in(me, dq, dk, dv, res1, weight):
    kind, refs = weight
    n = 3 * D
    count = copy_count(weight)

    def kernel(me_ref, q_ref, k_ref, v_ref, r_ref, *rest):
        w_refs, o_refs, (w_ref, sems) = rest[: len(refs)], rest[len(refs) : -2], rest[-2:]

        @pl.when(pl.program_id(0) == 0)
        def _():
            copies = weight_copies(kind, w_refs, (0, n // 2), (0, n), w_ref, sems, bits_of(me_ref))
            start_all(copies)
            wait_all(copies)

        total = r_ref[...] + nt(q_ref[...], w_ref[:, :D])
        total = total + nt(k_ref[...], w_ref[:, D : 2 * D])
        total = total + nt(v_ref[...], w_ref[:, 2 * D :])
        put_block(o_refs, pl.program_id(0), total.astype(BF))

    rows = dq.shape[0]
    blocks = rows // ROWS
    blk = pl.BlockSpec((ROWS, D), lambda i, me: (i, 0))
    return pl.pallas_call(
        kernel,
        grid_spec=pltpu.PrefetchScalarGridSpec(
            num_scalar_prefetch=1, grid=(rows // ROWS,),
            in_specs=[blk] * 4 + [ANY] * len(refs),
            out_specs=[pl.BlockSpec((ROWS, D), lambda i, me: (0, 0))] * blocks,
            scratch_shapes=[pltpu.VMEM((D, n), BF), pltpu.SemaphoreType.DMA((count,))]),
        out_shape=[jax.ShapeDtypeStruct((ROWS, D), BF)] * blocks,
        compiler_params=params(),
        cost_estimate=cost(9),
        name="grad_in",
    )(me, dq, dk, dv, res1, *refs)


def local(hidden_in, doc_starts, w_qkv, query_bias, value_bias, w_out, out_bias, norm1_gain,
          norm1_bias, w_up, up_bias, w_down, down_bias, norm2_gain, norm2_bias, cotangent):
    fsdp, sp = lax.axis_size("fsdp"), lax.axis_size("sp")
    seqs, span, _ = hidden_in.shape
    assert sp == 4 and seqs == sp and span * sp == SEQ and span == ROWS
    me = lax.axis_index("sp").astype(jnp.int32)
    core = me & 1
    row = lax.axis_index("fsdp").astype(jnp.int32)
    xb, zs = row & 1, fsdp // 2
    me1 = jnp.stack([me, xb])
    rows_d, rows_f = D // fsdp, FF // fsdp
    split = in_pieces(fsdp)

    def partner(v, bit):
        return lax.ppermute(v, "sp", [(i, i ^ bit) for i in range(sp)])

    def across(v):
        return lax.ppermute(v, "fsdp", [(i, i ^ 1) for i in range(fsdp)])

    lines = [[2 * z + b for z in range(zs)] for b in range(2)]

    def along(v):
        return lax.all_to_all(v, "fsdp", 0, 0, axis_index_groups=lines, tiled=True)

    def swap(parts):
        return [parts[0]] + [partner(parts[r], r) for r in (2, 3, 1)]

    def fetch(v):
        own, two, three, one = swap(deal(me1, v))
        return jnp.concatenate([own, one, two, three], 0)

    def deliver(parts):
        own, two, three, one = swap(parts)
        return place(me1, [own, one, two, three])

    def each(v):
        return jnp.broadcast_to(v[None], (zs,) + v.shape)

    def half_cols(w):
        return lax.dynamic_slice(w, (0, core * (w.shape[1] // 2)), (w.shape[0], w.shape[1] // 2))

    def spread(v):
        a = along(v)
        a = jnp.stack([a, across(a)])
        return a, partner(a, 1)

    small = [out_bias, norm1_gain, norm1_bias, down_bias, norm2_gain, norm2_bias, query_bias,
             value_bias, up_bias]
    x = fetch(hidden_in)
    if split:
        a1 = spread(pack(me1, w_qkv, small, zs))
        every = a1[0][:, :, rows_d:, :rows_f]
        every = jnp.where(xb == 0, every, every[::-1]).transpose(2, 1, 0, 3)
        every = every.astype(F32).reshape(16, fsdp, rows_f)
        table = every[:8, :, :rows_d].reshape(8, D)
        full_up_bias = every[8].reshape(1, FF)
        weight1 = ("cols", a1)
        weight2 = ("cols", spread(each(jnp.concatenate([half_cols(w_out), half_cols(w_up)], 1))))
        down = lax.dynamic_slice(w_down, (core * (rows_f // 2), 0), (rows_f // 2, D))
        weight3 = ("rows", spread(each(down)))
    else:
        every = lax.all_gather(jnp.concatenate(small), "fsdp", axis=0).astype(F32)
        table = every[:, : 8 * rows_d].reshape(fsdp, 8, rows_d).transpose(1, 0, 2).reshape(8, D)
        full_up_bias = every[:, 8 * rows_d :].reshape(1, FF)
        gather = lambda w: lax.all_gather(w, "fsdp", axis=0, tiled=True)
        weight1 = ("whole", (gather(w_qkv),))
        weight2 = ("whole", (gather(jnp.concatenate([w_out, w_up], 1)),))
        weight3 = ("whole", (gather(w_down),))
    g = fetch(cotangent)
    bias_row = jnp.concatenate([table[6:7], jnp.zeros((1, D), F32), table[7:8]], 1)

    starts = lax.dynamic_slice(doc_starts, (me, 0), (1, doc_starts.shape[1]))
    order = jnp.arange(SEQ, dtype=jnp.int32)
    position = ((order // span) ^ me) * span + order % span
    seg = jnp.sum((position[:, None] >= starts).astype(jnp.int32), -1)
    seg_col, seg_row = seg[:, None], seg[None, :]

    qkv = project(me1, x, weight1, bias_row)
    context = ()
    per = PAIRS // PARTS
    for i in range(PARTS):
        context = attend(qkv, seg_col, seg_row, i * per, per, context)
    context, lse = context
    (*out, act, gpre, low1, gffn, gattn, res1, gctx, sums, up_sums) = middle(
        me1, context, x, g, table, full_up_bias, weight2, weight3)
    layer_out = deliver(out)

    def add(a, b):
        return (a.astype(F32) + b.astype(F32)).astype(BF)

    def join(mine, other, axis):
        return jnp.where(core == 0, jnp.concatenate([mine, other], axis),
                         jnp.concatenate([other, mine], axis))

    def reduce_part(send, keep):
        other = partner(send, 1)
        cut = lambda v, b: lax.dynamic_index_in_dim(v.reshape((zs, 2) + v.shape[1:]), b, 1, False)
        theirs = add(cut(keep, 1 - xb), cut(other, 1 - xb))
        mine = add(add(cut(keep, xb), cut(other, xb)), across(theirs))
        total = jnp.sum(along(mine).astype(F32), 0).astype(BF)
        total = add(total, partner(total, 2))
        return total, partner(total, 1)

    def scatter(v):
        part = lax.psum_scatter(v, "fsdp", scatter_dimension=0, tiled=True)
        return lax.psum(part, "sp").astype(F32)

    down_parts = grad_down(me1, act, gffn, fsdp)
    wide_parts = grad_up_out(me1, low1, gpre, context, gattn)
    if split:
        down = reduce_part(*down_parts)
        wide = reduce_part(*[v.reshape(fsdp, rows_d, -1) for v in wide_parts])
    grads = ()
    for i in range(PARTS):
        grads = attend_back(qkv, context, gctx, lse, seg_col, seg_row, i * per, per, grads)
    dq, dk, dv, bias_sums = grads
    qkv_parts = grad_qkv(me1, x, dq, dk, dv, sums, up_sums, bias_sums, fsdp)
    if split:
        qkv_sum = reduce_part(*qkv_parts)
    dx = grad_in(me1, dq, dk, dv, res1, weight1)
    grad_input = deliver(dx)

    if split:
        both = lambda pair, axis: join(pair[0], pair[1], axis).astype(F32)
        grad_down_w = both(down, 0)
        w1 = D // 2
        grad_out = both([v[:, :w1] for v in wide], 1)
        grad_up = both([v[:, w1:] for v in wide], 1)
        grad_q = both([v[:rows_d] for v in qkv_sum], 1)
        tail = qkv_sum[0][rows_d:].astype(F32)
        g2, b2, db, g1, b1, ob, qb, vb = [tail[i, :rows_d] for i in range(8)]
        ub = tail[8, :rows_f]
    else:
        grad_down_w = scatter(join(*down_parts[::-1], 1).reshape(FF, D).astype(F32))
        wide = scatter(join(*wide_parts[::-1], 1).astype(F32))
        w1, w2 = D // 2, FF // 2
        grad_out = jnp.concatenate([wide[:, :w1], wide[:, w1 + w2 : 2 * w1 + w2]], 1)
        grad_up = jnp.concatenate([wide[:, w1 : w1 + w2], wide[:, 2 * w1 + w2 :]], 1)
        grad_q = scatter(join(*[v[:, :rows_d] for v in qkv_parts[::-1]], 2).reshape(D, 3 * D).astype(F32))
        by_dest = jnp.concatenate([sums[:6], bias_sums[:2]], 0).reshape(8, fsdp, rows_d)
        by_dest = by_dest.transpose(1, 0, 2).reshape(fsdp, 8 * rows_d)
        extra = jnp.concatenate([by_dest, up_sums[0].reshape(fsdp, rows_f)], 1)
        tail = scatter(extra).reshape(-1)
        g2, b2, db, g1, b1, ob, qb, vb = [tail[i * rows_d : (i + 1) * rows_d] for i in range(8)]
        ub = tail[8 * rows_d :]
    return (layer_out, grad_input, grad_q, qb, vb, grad_out, ob, g1, b1, grad_up, ub, grad_down_w,
            db, g2, b2)


PARTS = 3


def in_pieces(fsdp):
    return D // fsdp % 32 == 0 and FF // fsdp % 32 == 0


def solution(mesh):
    tok = P("fsdp", "sp", None)
    mat, vec = P("fsdp", None), P("fsdp")
    in_specs = (tok, mat, mat, vec, vec, mat, vec, vec, vec, mat, vec, mat, vec, vec, vec, tok)
    out_specs = (tok, tok, mat, vec, vec, mat, vec, vec, vec, mat, vec, mat, vec, vec, vec)

    return jax.shard_map(local, mesh=mesh, in_specs=in_specs, out_specs=out_specs, check_vma=False)
```

```python
import jax
import jax.numpy as jnp
from jax import lax
from jax.experimental import pallas as pl
from jax.experimental.pallas import tpu as pltpu
from jax.sharding import PartitionSpec as P


D = 768
H = 12
HD = 64
FF = 3072
SEQ = 1024
PAIRS = H // 2
EPS = 1e-05
MASKED = -1000000000.0
SCALE = HD ** (-0.5)
BF = jnp.bfloat16
F32 = jnp.float32
ROWS = 256
MIB = 1 << 20


ERFC = (
    0.2820844758103095,
    0.28240952292464144,
    0.24285408258103366,
    0.20367679547693512,
    -0.028968306758876145,
    0.2814702272328375,
    -0.49017537256556365,
    0.28601194065835034,
    -0.059363409284156475,
)


def nn(a, b):
    return lax.dot_general(a, b, (((1,), (0,)), ((), ())), preferred_element_type=F32)


def nt(a, b):
    return lax.dot_general(a, b, (((1,), (1,)), ((), ())), preferred_element_type=F32)


def tn(a, b):
    return lax.dot_general(a, b, (((0,), (0,)), ((), ())), preferred_element_type=F32)


def gelu_with_slope(x):
    z = jnp.abs(x) * 0.7071067811865476
    t = 1.0 / (1.0 + 0.5 * z)
    e = jnp.exp(-0.5 * (x * x))
    poly = jnp.full_like(t, 0.5 * ERFC[-1])
    for c in ERFC[-2::-1]:
        poly = poly * t + 0.5 * c
    tail = poly * t * e
    cdf = jnp.where(x >= 0, 1.0 - tail, tail)
    return x * cdf, cdf + x * (e * 0.3989422804014327)


def norm_rows(v):
    c = v - jnp.mean(v, -1, keepdims=True)
    r = lax.rsqrt(jnp.mean(c * c, -1, keepdims=True) + EPS)
    return c * r, r


def norm_rows_back(a, xhat, rstd):
    return rstd * (a - jnp.mean(a, -1, keepdims=True) - xhat * jnp.mean(a * xhat, -1, keepdims=True))


def piece_copies(pieces, by_rows, cols, dst, sems, core, x_bit):
    copies = []
    lo, nc = cols
    for rc, ref in enumerate(pieces):
        _, count, nr, _ = ref.shape
        nr -= nr % (D // 8 // 2) if not by_rows else 0
        row0 = nr * lax.bitwise_xor(core, rc) if by_rows else 0
        col0 = 0 if by_rows else nc * lax.bitwise_xor(core, rc)
        stride = nr * (2 if by_rows else 1)
        for rx in range(2):
            for z in range(count):
                row = row0 + stride * (2 * z + lax.bitwise_xor(x_bit, rx))
                copies.append(
                    pltpu.make_async_copy(
                        ref.at[rx, z, pl.ds(0, nr), pl.ds(lo, nc)],
                        dst.at[
                            pl.ds(pl.multiple_of(row, nr), nr),
                            pl.ds(0 if by_rows else pl.multiple_of(col0, nc), nc),
                        ],
                        sems.at[(rc * 2 + rx) * count + z],
                    )
                )
    return copies


def whole_copies(ref, cols, dst, sems):
    lo, nc = cols
    return [pltpu.make_async_copy(ref.at[:, pl.ds(lo, nc)], dst, sems.at[0])]


def weight_copies(kind, refs, cols, full_cols, dst, sems, bits):
    if kind == "whole":
        return whole_copies(refs[0], full_cols, dst, sems)
    return piece_copies(refs, kind == "rows", full_cols if kind == "rows" else cols, dst, sems, *bits)


def copy_count(weight):
    kind, refs = weight
    return 1 if kind == "whole" else 4 * refs[0].shape[1]


def put_block(refs, step, value):
    for r, ref in enumerate(refs):
        @pl.when(step == r)
        def _():
            ref[...] = value


def start_all(copies):
    for c in copies:
        c.start()


def wait_all(copies):
    for c in copies:
        c.wait()


ANY = pl.BlockSpec(memory_space=pl.ANY)


def cost(us):
    return pl.CostEstimate(flops=int(us * 1e9), bytes_accessed=1 << 20, transcendentals=0)


def params(vmem=58):
    return pltpu.CompilerParams(
        dimension_semantics=("arbitrary",), vmem_limit_bytes=vmem * MIB
    )


def bits_of(me_ref):
    return lax.bitwise_and(me_ref[0], 1), me_ref[1]


def pack(me, w, vectors, copies):
    rows, width = w.shape[0], w.shape[1] // 2

    def kernel(me_ref, w_ref, *rest):
        v_refs, o_ref = rest[:-1], rest[-1]
        for z in range(copies):
            o_ref[z, :rows, :] = w_ref[...]
            o_ref[z, rows:, :] = jnp.zeros((16, width), BF)
        for i, v in enumerate(v_refs):
            for z in range(copies):
                o_ref[z, rows + i : rows + i + 1, : v.shape[0]] = v[...].reshape(1, -1)

    one = lambda v: pl.BlockSpec(v.shape, lambda i, me: (0,))
    return pl.pallas_call(
        kernel,
        grid_spec=pltpu.PrefetchScalarGridSpec(
            num_scalar_prefetch=1,
            grid=(1,),
            in_specs=[pl.BlockSpec((rows, width), lambda i, me: (0, lax.bitwise_and(me[0], 1)))]
            + [one(v) for v in vectors],
            out_specs=pl.BlockSpec((copies, rows + 16, width), lambda i, me: (0, 0, 0)),
        ),
        out_shape=jax.ShapeDtypeStruct((copies, rows + 16, width), BF),
        compiler_params=params(),
        cost_estimate=cost(2),
        name="pack",
    )(me, w, *vectors)


def block_at(r):
    return pl.BlockSpec((None, ROWS, D), lambda i, me: (lax.bitwise_xor(me[0], r), 0, 0))


WHOLE = pl.BlockSpec((ROWS, D), lambda i, me: (0, 0))


def deal(me, v):
    away = v.shape[0] - 1

    def kernel(me_ref, *refs):
        for r in range(away):
            refs[away + r][...] = refs[r][...]

    return pl.pallas_call(
        kernel,
        grid_spec=pltpu.PrefetchScalarGridSpec(
            num_scalar_prefetch=1, grid=(1,),
            in_specs=[block_at(r + 1) for r in range(away)],
            out_specs=[WHOLE] * away),
        out_shape=[jax.ShapeDtypeStruct((ROWS, D), v.dtype)] * away,
        compiler_params=params(),
        cost_estimate=cost(2),
        name="deal",
    )(me, *([v] * away))


def place(me, parts):
    n = len(parts)

    def kernel(me_ref, *refs):
        for r in range(n):
            @pl.when(pl.program_id(0) == r)
            def _():
                refs[n][...] = refs[r][...]

    return pl.pallas_call(
        kernel,
        grid_spec=pltpu.PrefetchScalarGridSpec(
            num_scalar_prefetch=1, grid=(n,),
            in_specs=[WHOLE] * n,
            out_specs=pl.BlockSpec((None, ROWS, D), lambda i, me: (lax.bitwise_xor(me[0], i), 0, 0))),
        out_shape=jax.ShapeDtypeStruct((n, ROWS, D), parts[0].dtype),
        compiler_params=params(),
        cost_estimate=cost(2),
        name="place",
    )(me, *parts)


def own_and_near(v, parts):
    return [v] + list(parts), [block_at(0)] + [WHOLE] * len(parts)


def get_block(refs, step, into):
    for r, ref in enumerate(refs):
        @pl.when(step == r)
        def _():
            into[...] = ref[...]


def project(me, x_own, x_near, weight, bias_row):
    kind, refs = weight
    n = 3 * D
    count = copy_count(weight)

    x_args, x_specs = own_and_near(x_own, x_near)
    blocks = len(x_args)

    def kernel(me_ref, b_ref, *rest):
        x_refs, w_refs, (o_ref, x_ref, w_ref, sems) = rest[:blocks], rest[blocks:-4], rest[-4:]
        get_block(x_refs, pl.program_id(0), x_ref)

        @pl.when(pl.program_id(0) == 0)
        def _():
            copies = weight_copies(kind, w_refs, (0, n // 2), (0, n), w_ref, sems, bits_of(me_ref))
            start_all(copies)
            wait_all(copies)

        xv = x_ref[...]
        for lo in range(0, n, D):
            o_ref[:, lo : lo + D] = (
                nn(xv, w_ref[:, lo : lo + D]) + b_ref[:, lo : lo + D]
            ).astype(BF)

    rows = ROWS * blocks
    return pl.pallas_call(
        kernel,
        grid_spec=pltpu.PrefetchScalarGridSpec(
            num_scalar_prefetch=1,
            grid=(blocks,),
            in_specs=[pl.BlockSpec((1, n), lambda i, me: (0, 0))] + x_specs + [ANY] * len(refs),
            out_specs=[pl.BlockSpec((ROWS, n), lambda i, me: (i, 0)),
                       pl.BlockSpec((ROWS, D), lambda i, me: (i, 0))],
            scratch_shapes=[pltpu.VMEM((D, n), BF), pltpu.SemaphoreType.DMA((count,))],
        ),
        out_shape=[jax.ShapeDtypeStruct((rows, n), BF), jax.ShapeDtypeStruct((rows, D), BF)],
        compiler_params=params(),
        cost_estimate=cost(9),
        name="project",
    )(me, bias_row, *x_args, *refs)


def attend(qkv, seg_col, seg_row, first, count, before):
    chunk = 256

    def kernel(q_ref, k_ref, v_ref, sc_ref, sr_ref, *rest):
        o_ref, lse_ref = rest[-2:]
        lane = lax.broadcasted_iota(jnp.int32, (1, 2 * HD), 1)
        k = k_ref[...]
        vt = v_ref[...].T
        seg_k = sc_ref[...]
        for c in range(SEQ // chunk):
            at = pl.ds(c * chunk, chunk)
            q = q_ref[at, :] * jnp.asarray(SCALE, BF)
            same = seg_k == sr_ref[:, at]
            outs = []
            for h in range(2):
                mine = (lane < HD) if h == 0 else (lane >= HD)
                s = nt(k, jnp.where(mine, q, jnp.zeros_like(q)))
                s = jnp.where(same, s, MASKED)
                m = jnp.max(s, 0, keepdims=True)
                p = jnp.exp(s - m)
                l = jnp.sum(p, 0, keepdims=True)
                lse_ref[0, h : h + 1, at] = m + jnp.log(l)
                o = nn(vt, p.astype(BF))
                outs.append(o[h * HD : (h + 1) * HD] * (1.0 / l))
            o_ref[at, :] = jnp.concatenate(outs, 0).T.astype(BF)

    spec = lambda off: pl.BlockSpec((SEQ, 2 * HD), lambda i: (0, i + off + first))
    full = lambda s: pl.BlockSpec(s, lambda i: (0,) * len(s))
    return pl.pallas_call(
        kernel,
        grid=(count,),
        in_specs=[spec(0), spec(PAIRS), spec(2 * PAIRS), full((SEQ, 1)), full((1, SEQ))]
        + [ANY] * len(before),
        out_specs=[spec(0), pl.BlockSpec((1, 8, SEQ), lambda i: (i + first, 0, 0))],
        input_output_aliases={5 + i: i for i in range(len(before))},
        out_shape=[
            jax.ShapeDtypeStruct((SEQ, D), BF),
            jax.ShapeDtypeStruct((PAIRS, 8, SEQ), F32),
        ],
        compiler_params=params(),
        cost_estimate=cost(6 * count),
        name="attend",
    )(qkv, qkv, qkv, seg_col, seg_row, *before)


def attend_back(qkv, context, grad_context, lse, seg_col, seg_row, start, count, before):
    chunk = 256

    def kernel(q_ref, k_ref, v_ref, o_ref, g_ref, lse_ref, sc_ref, sr_ref, *rest):
        dq_ref, dk_ref, dv_ref, sum_ref, acc_ref, kt_ref = rest[-6:]
        lane = lax.broadcasted_iota(jnp.int32, (1, 2 * HD), 1)
        first = lane < HD
        q = q_ref[...] * jnp.asarray(SCALE, BF)
        g = g_ref[...]
        zero = jnp.zeros_like(q)
        prod = (g.astype(F32) * o_ref[...].astype(F32)).T
        inner = [jnp.sum(prod[h * HD : (h + 1) * HD], 0, keepdims=True) for h in range(2)]
        qm = [jnp.where(first, q, zero), jnp.where(first, zero, q)]
        gm = [jnp.where(first, g, zero), jnp.where(first, zero, g)]
        seg_q = sr_ref[...]
        kt_ref[...] = k_ref[...].T
        acc_ref[...] = jnp.zeros_like(acc_ref)
        dv_total = jnp.zeros((1, 2 * HD), F32)
        for c in range(SEQ // chunk):
            at = pl.ds(c * chunk, chunk)
            k = k_ref[at, :]
            v = v_ref[at, :]
            same = sc_ref[at, :] == seg_q
            dks, dvs = [], []
            for h in range(2):
                s = jnp.where(same, nt(k, qm[h]), MASKED)
                p = jnp.exp(s - lse_ref[0, h : h + 1, :])
                ds = (p * (nt(v, gm[h]) - inner[h])).astype(BF)
                dvs.append(nn(p.astype(BF), g))
                dks.append(nn(ds, q))
                half = pl.ds(h * HD, HD)
                acc_ref[half, :] += nn(kt_ref[half, at], ds)
            dk_ref[at, :] = jnp.where(first, dks[0], dks[1]).astype(BF)
            dv = jnp.where(first, dvs[0], dvs[1]).astype(BF)
            dv_ref[at, :] = dv
            dv_total += jnp.sum(dv.astype(F32), 0, keepdims=True)
        dq = (acc_ref[...].T * SCALE).astype(BF)
        dq_ref[...] = dq
        sum_ref[0:1, :] = jnp.sum(dq.astype(F32), 0, keepdims=True)
        sum_ref[1:2, :] = dv_total

    spec = lambda off: pl.BlockSpec((SEQ, 2 * HD), lambda i: (0, i + off + start))
    full = lambda s: pl.BlockSpec(s, lambda i: (0,) * len(s))
    return pl.pallas_call(
        kernel,
        grid=(count,),
        in_specs=[spec(0), spec(PAIRS), spec(2 * PAIRS), spec(0), spec(0),
                  pl.BlockSpec((1, 8, SEQ), lambda i: (i + start, 0, 0)), full((SEQ, 1)),
                  full((1, SEQ))] + [ANY] * len(before),
        out_specs=[spec(0), spec(0), spec(0), pl.BlockSpec((8, 2 * HD), lambda i: (0, i + start))],
        input_output_aliases={8 + i: i for i in range(len(before))},
        out_shape=[jax.ShapeDtypeStruct((SEQ, D), BF)] * 3 + [jax.ShapeDtypeStruct((8, D), F32)],
        scratch_shapes=[pltpu.VMEM((2 * HD, SEQ), F32), pltpu.VMEM((2 * HD, SEQ), BF)],
        compiler_params=params(),
        cost_estimate=cost(6 * count),
        name="attend_back",
    )(qkv, qkv, qkv, context, grad_context, lse, seg_col, seg_row, *before)


def middle(me, context, x, g_own, g_near, vectors, up_bias, weight2, weight3):
    kind2, refs2 = weight2
    kind3, refs3 = weight3
    count = copy_count(weight2)
    blocks = x.shape[0] // ROWS

    g_args, g_specs = own_and_near(g_own, g_near)

    def kernel(me_ref, c_ref, x_ref, vec_ref, ub_ref, *rest):
        g_refs, rest = rest[:blocks], rest[blocks:]
        w2, w3 = rest[: len(refs2)], rest[len(refs2) : len(refs2) + len(refs3)]
        o_refs = rest[len(refs2) + len(refs3) :][:blocks]
        (act_ref, gpre_ref, n1_ref, gffn_ref, gattn_ref, gres_ref, gctx_ref,
         sum_ref, usum_ref, wo, wu, wd, slope, g_ref, s_o, s_u, s_d) = rest[len(refs2) + len(refs3) + blocks :]
        step = pl.program_id(0)
        get_block(g_refs, step, g_ref)
        bits = bits_of(me_ref)
        co = weight_copies(kind2, w2, (0, D // 2), (0, D), wo, s_o, bits)
        cu = weight_copies(kind2, w2, (D // 2, FF // 2), (D, FF), wu, s_u, bits)
        cd = weight_copies(kind3, w3, None, (0, D), wd, s_d, bits)

        @pl.when(step == 0)
        def _():
            start_all(co)
            start_all(cu)
            start_all(cd)
            sum_ref[...] = jnp.zeros_like(sum_ref)
            usum_ref[...] = jnp.zeros_like(usum_ref)
            wait_all(co)

        out_bias, gain1, shift1 = vec_ref[0:1], vec_ref[1:2], vec_ref[2:3]
        down_bias, gain2, shift2 = vec_ref[3:4], vec_ref[4:5], vec_ref[5:6]
        attn = nn(c_ref[...], wo[...]) + out_bias
        xhat1, rstd1 = norm_rows(x_ref[...].astype(F32) + attn)
        normed1 = xhat1 * gain1 + shift1
        low1 = normed1.astype(BF)
        n1_ref[...] = low1

        @pl.when(step == 0)
        def _():
            wait_all(cu)
            wait_all(cd)

        ffn = jnp.zeros((ROWS, D), F32)
        for lo in range(0, FF, D):
            at = slice(lo, lo + D)
            pre = nn(low1, wu[:, at]) + ub_ref[:, at]
            act, sl = gelu_with_slope(pre)
            act = act.astype(BF)
            act_ref[:, at] = act
            slope[:, at] = sl
            ffn = ffn + nn(act, wd[at, :])
        xhat2, rstd2 = norm_rows(normed1 + (ffn + down_bias))
        out = (xhat2 * gain2 + shift2).astype(BF)
        put_block(o_refs, step, out)
        gr = g_ref[...].astype(F32)
        res2 = norm_rows_back(gr * gain2, xhat2, rstd2)
        gffn = res2.astype(BF)
        gffn_ref[...] = gffn
        rs = lambda v: jnp.sum(v, 0, keepdims=True)
        sum_ref[0:1] += rs(gr * xhat2)
        sum_ref[1:2] += rs(gr)
        sum_ref[2:3] += rs(gffn.astype(F32))
        gn1 = res2
        for lo in range(0, FF, D):
            at = slice(lo, lo + D)
            gpre = (nt(gffn, wd[at, :]) * slope[:, at]).astype(BF)
            gpre_ref[:, at] = gpre
            usum_ref[0:1, at] += rs(gpre.astype(F32))
            gn1 = gn1 + nt(gpre, wu[:, at])
        sum_ref[3:4] += rs(gn1 * xhat1)
        sum_ref[4:5] += rs(gn1)
        res1 = norm_rows_back(gn1 * gain1, xhat1, rstd1)
        gres_ref[...] = res1
        gattn = res1.astype(BF)
        gattn_ref[...] = gattn
        sum_ref[5:6] += rs(gattn.astype(F32))
        gctx_ref[...] = nt(gattn, wo[...]).astype(BF)

    rows = x.shape[0]
    blk = lambda n: pl.BlockSpec((ROWS, n), lambda i, me: (i, 0))
    full = lambda s: pl.BlockSpec(s, lambda i, me: (0,) * len(s))
    sd = jax.ShapeDtypeStruct
    return pl.pallas_call(
        kernel,
        grid_spec=pltpu.PrefetchScalarGridSpec(
            num_scalar_prefetch=1,
            grid=(rows // ROWS,),
            in_specs=[blk(D), blk(D), full((8, D)), full((1, FF))] + g_specs
            + [ANY] * (len(refs2) + len(refs3)),
            out_specs=[full((ROWS, D))] * blocks + [blk(FF), blk(FF), blk(D), blk(D), blk(D), blk(D), blk(D),
                       full((8, D)), full((8, FF))],
            scratch_shapes=[
                pltpu.VMEM((D, D), BF), pltpu.VMEM((D, FF), BF), pltpu.VMEM((FF, D), BF),
                pltpu.VMEM((ROWS, FF), F32), pltpu.VMEM((ROWS, D), BF),
                pltpu.SemaphoreType.DMA((count,)), pltpu.SemaphoreType.DMA((count,)),
                pltpu.SemaphoreType.DMA((count,)),
            ],
        ),
        out_shape=[sd((ROWS, D), BF)] * blocks + [sd((rows, FF), BF), sd((rows, FF), BF), sd((rows, D), BF),
                   sd((rows, D), BF), sd((rows, D), BF), sd((rows, D), F32), sd((rows, D), BF),
                   sd((8, D), F32), sd((8, FF), F32)],
        compiler_params=params(),
        cost_estimate=cost(48),
        name="middle",
    )(me, context, x, vectors, up_bias, *g_args, *refs2, *refs3)


def grad_down(me, act, grad_ffn, fsdp):
    per = FF // fsdp
    steps = 8
    width = FF // steps
    inner = width // per

    def kernel(me_ref, a_ref, g_ref, send_ref, keep_ref, acc_ref):
        core, _ = bits_of(me_ref)
        acc_ref[...] = tn(a_ref[...], g_ref[...])
        n = per // 2
        for i in range(inner):
            take = lambda b: acc_ref[pl.ds(pl.multiple_of(i * per + n * b, n), n), :].astype(BF)
            send_ref[i] = take(1 - core)
            keep_ref[i] = take(core)

    rows = act.shape[0]
    out = jax.ShapeDtypeStruct((fsdp, per // 2, D), BF)
    ospec = pl.BlockSpec((inner, per // 2, D), lambda i, me: (i, 0, 0))
    return pl.pallas_call(
        kernel,
        grid_spec=pltpu.PrefetchScalarGridSpec(
            num_scalar_prefetch=1,
            grid=(steps,),
            in_specs=[pl.BlockSpec((rows, width), lambda i, me: (0, i)),
                      pl.BlockSpec((rows, D), lambda i, me: (0, 0))],
            out_specs=[ospec, ospec],
            scratch_shapes=[pltpu.VMEM((width, D), F32)],
        ),
        out_shape=[out, out],
        compiler_params=params(),
        cost_estimate=cost(12),
        name="grad_down",
    )(me, act, grad_ffn)


def halves_out(rows, width):
    specs = [pl.BlockSpec((rows, width), lambda i, me: (0, 0))] * 2
    shapes = [jax.ShapeDtypeStruct((rows, width), BF)] * 2
    return specs, shapes


def half_of(i, core):
    return jnp.where(i == 0, 1 - core, core)


def grad_up_out(me, low1, grad_pre, context, grad_attn):
    wu, wo = FF // 2, D // 2

    def kernel(me_ref, l_ref, p_ref, c_ref, a_ref, send_ref, keep_ref):
        def fill(o_ref):
            o_ref[:, :wo] = tn(c_ref[...], a_ref[...]).astype(BF)
            low = l_ref[...]
            for lo in range(0, wu, D):
                o_ref[:, wo + lo : wo + lo + D] = tn(low, p_ref[:, lo : lo + D]).astype(BF)

        pl.when(pl.program_id(0) == 0)(lambda: fill(send_ref))
        pl.when(pl.program_id(0) == 1)(lambda: fill(keep_ref))

    rows = low1.shape[0]
    half = lambda n: pl.BlockSpec(
        (rows, n), lambda i, me: (0, half_of(i, lax.bitwise_and(me[0], 1))))
    full = pl.BlockSpec((rows, D), lambda i, me: (0, 0))
    specs, shapes = halves_out(D, wu + wo)
    return pl.pallas_call(
        kernel,
        grid_spec=pltpu.PrefetchScalarGridSpec(
            num_scalar_prefetch=1, grid=(2,),
            in_specs=[full, half(wu), full, half(wo)], out_specs=specs),
        out_shape=shapes,
        compiler_params=params(),
        cost_estimate=cost(12),
        name="grad_up_out",
    )(me, low1, grad_pre, context, grad_attn)


def grad_qkv(me, x, dq, dk, dv, sums, up_sums, bias_sums, fsdp):
    w = 3 * D // 2
    per, per_up = D // fsdp, FF // fsdp
    tall = per + 16

    def kernel(me_ref, x_ref, q_ref, k_ref, v_ref, s_ref, u_ref, b_ref, send_ref, keep_ref):
        core, _ = bits_of(me_ref)

        def put(o_ref, lo, val):
            val = val.astype(BF)
            for d in range(fsdp):
                o_ref[d, :per, lo : lo + val.shape[1]] = val[d * per : (d + 1) * per]

        def fill(o_ref, b):
            @pl.when(b == 0)
            def _():
                put(o_ref, 0, tn(x_ref[...], q_ref[...]))
                put(o_ref, D, tn(x_ref[...], k_ref[:, : D // 2]))

            @pl.when(b == 1)
            def _():
                put(o_ref, 0, tn(x_ref[...], k_ref[:, D // 2 :]))
                put(o_ref, D // 2, tn(x_ref[...], v_ref[...]))

            rows = jnp.concatenate([s_ref[0:6], b_ref[0:2]], 0)
            for d in range(fsdp):
                o_ref[d, per:, :] = jnp.zeros((16, w), BF)
                o_ref[d, per : per + 8, :per] = rows[:, d * per : (d + 1) * per].astype(BF)
                o_ref[d, per + 8 : per + 9, :per_up] = u_ref[0:1, d * per_up : (d + 1) * per_up].astype(BF)

        pl.when(pl.program_id(0) == 0)(lambda: fill(send_ref, 1 - core))
        pl.when(pl.program_id(0) == 1)(lambda: fill(keep_ref, core))

    rows = x.shape[0]
    full = lambda s: pl.BlockSpec(s, lambda i, me: (0, 0))
    return pl.pallas_call(
        kernel,
        grid_spec=pltpu.PrefetchScalarGridSpec(
            num_scalar_prefetch=1, grid=(2,),
            in_specs=[full((rows, D))] * 4 + [full((8, D)), full((8, FF)), full((8, D))],
            out_specs=[pl.BlockSpec((fsdp, tall, w), lambda i, me: (0, 0, 0))] * 2),
        out_shape=[jax.ShapeDtypeStruct((fsdp, tall, w), BF)] * 2,
        compiler_params=params(),
        cost_estimate=cost(9),
        name="grad_qkv",
    )(me, x, dq, dk, dv, sums, up_sums, bias_sums)


def grad_in(me, dq, dk, dv, res1, weight):
    kind, refs = weight
    n = 3 * D
    count = copy_count(weight)

    def kernel(me_ref, q_ref, k_ref, v_ref, r_ref, *rest):
        w_refs, o_refs, (w_ref, sems) = rest[: len(refs)], rest[len(refs) : -2], rest[-2:]

        @pl.when(pl.program_id(0) == 0)
        def _():
            copies = weight_copies(kind, w_refs, (0, n // 2), (0, n), w_ref, sems, bits_of(me_ref))
            start_all(copies)
            wait_all(copies)

        total = r_ref[...] + nt(q_ref[...], w_ref[:, :D])
        total = total + nt(k_ref[...], w_ref[:, D : 2 * D])
        total = total + nt(v_ref[...], w_ref[:, 2 * D :])
        put_block(o_refs, pl.program_id(0), total.astype(BF))

    rows = dq.shape[0]
    blocks = rows // ROWS
    blk = pl.BlockSpec((ROWS, D), lambda i, me: (i, 0))
    return pl.pallas_call(
        kernel,
        grid_spec=pltpu.PrefetchScalarGridSpec(
            num_scalar_prefetch=1, grid=(rows // ROWS,),
            in_specs=[blk] * 4 + [ANY] * len(refs),
            out_specs=[pl.BlockSpec((ROWS, D), lambda i, me: (0, 0))] * blocks,
            scratch_shapes=[pltpu.VMEM((D, n), BF), pltpu.SemaphoreType.DMA((count,))]),
        out_shape=[jax.ShapeDtypeStruct((ROWS, D), BF)] * blocks,
        compiler_params=params(),
        cost_estimate=cost(9),
        name="grad_in",
    )(me, dq, dk, dv, res1, *refs)


def local(hidden_in, doc_starts, w_qkv, query_bias, value_bias, w_out, out_bias, norm1_gain,
          norm1_bias, w_up, up_bias, w_down, down_bias, norm2_gain, norm2_bias, cotangent):
    fsdp, sp = lax.axis_size("fsdp"), lax.axis_size("sp")
    seqs, span, _ = hidden_in.shape
    assert sp == 4 and seqs == sp and span * sp == SEQ and span == ROWS
    me = lax.axis_index("sp").astype(jnp.int32)
    core = me & 1
    row = lax.axis_index("fsdp").astype(jnp.int32)
    xb, zs = row & 1, fsdp // 2
    me1 = jnp.stack([me, xb])
    rows_d, rows_f = D // fsdp, FF // fsdp
    split = in_pieces(fsdp)

    def partner(v, bit):
        return lax.ppermute(v, "sp", [(i, i ^ bit) for i in range(sp)])

    def across(v):
        return lax.ppermute(v, "fsdp", [(i, i ^ 1) for i in range(fsdp)])

    lines = [[2 * z + b for z in range(zs)] for b in range(2)]

    def along(v):
        return lax.all_to_all(v, "fsdp", 0, 0, axis_index_groups=lines, tiled=True)

    def swap(parts):
        two, three, one = [partner(parts[r - 1], r) for r in (2, 3, 1)]
        return [one, two, three]

    def fetch(v):
        return swap(deal(me1, v))

    def deliver(parts):
        return place(me1, [parts[0]] + swap(parts[1:]))

    def each(v):
        return jnp.broadcast_to(v[None], (zs,) + v.shape)

    def half_cols(w):
        return lax.dynamic_slice(w, (0, core * (w.shape[1] // 2)), (w.shape[0], w.shape[1] // 2))

    def spread(v):
        a = along(v)
        a = jnp.stack([a, across(a)])
        return a, partner(a, 1)

    small = [out_bias, norm1_gain, norm1_bias, down_bias, norm2_gain, norm2_bias, query_bias,
             value_bias, up_bias]
    x_near = fetch(hidden_in)
    if split:
        a1 = spread(pack(me1, w_qkv, small, zs))
        every = a1[0][:, :, rows_d:, :rows_f]
        every = jnp.where(xb == 0, every, every[::-1]).transpose(2, 1, 0, 3)
        every = every.astype(F32).reshape(16, fsdp, rows_f)
        table = every[:8, :, :rows_d].reshape(8, D)
        full_up_bias = every[8].reshape(1, FF)
        weight1 = ("cols", a1)
        weight2 = ("cols", spread(each(jnp.concatenate([half_cols(w_out), half_cols(w_up)], 1))))
        down = lax.dynamic_slice(w_down, (core * (rows_f // 2), 0), (rows_f // 2, D))
        weight3 = ("rows", spread(each(down)))
    else:
        every = lax.all_gather(jnp.concatenate(small), "fsdp", axis=0).astype(F32)
        table = every[:, : 8 * rows_d].reshape(fsdp, 8, rows_d).transpose(1, 0, 2).reshape(8, D)
        full_up_bias = every[:, 8 * rows_d :].reshape(1, FF)
        gather = lambda w: lax.all_gather(w, "fsdp", axis=0, tiled=True)
        weight1 = ("whole", (gather(w_qkv),))
        weight2 = ("whole", (gather(jnp.concatenate([w_out, w_up], 1)),))
        weight3 = ("whole", (gather(w_down),))
    g_near = fetch(cotangent)
    bias_row = jnp.concatenate([table[6:7], jnp.zeros((1, D), F32), table[7:8]], 1)

    starts = lax.dynamic_slice(doc_starts, (me, 0), (1, doc_starts.shape[1]))
    order = jnp.arange(SEQ, dtype=jnp.int32)
    position = ((order // span) ^ me) * span + order % span
    seg = jnp.sum((position[:, None] >= starts).astype(jnp.int32), -1)
    seg_col, seg_row = seg[:, None], seg[None, :]

    qkv, x = project(me1, hidden_in, x_near, weight1, bias_row)
    context = ()
    per = PAIRS // PARTS
    for i in range(PARTS):
        context = attend(qkv, seg_col, seg_row, i * per, per, context)
    context, lse = context
    (*out, act, gpre, low1, gffn, gattn, res1, gctx, sums, up_sums) = middle(
        me1, context, x, cotangent, g_near, table, full_up_bias, weight2, weight3)
    layer_out = deliver(out)

    def add(a, b):
        return (a.astype(F32) + b.astype(F32)).astype(BF)

    def join(mine, other, axis):
        return jnp.where(core == 0, jnp.concatenate([mine, other], axis),
                         jnp.concatenate([other, mine], axis))

    def reduce_part(send, keep):
        other = partner(send, 1)
        cut = lambda v, b: lax.dynamic_index_in_dim(v.reshape((zs, 2) + v.shape[1:]), b, 1, False)
        theirs = add(cut(keep, 1 - xb), cut(other, 1 - xb))
        mine = add(add(cut(keep, xb), cut(other, xb)), across(theirs))
        total = jnp.sum(along(mine).astype(F32), 0).astype(BF)
        total = add(total, partner(total, 2))
        return total, partner(total, 1)

    def scatter(v):
        part = lax.psum_scatter(v, "fsdp", scatter_dimension=0, tiled=True)
        return lax.psum(part, "sp").astype(F32)

    down_parts = grad_down(me1, act, gffn, fsdp)
    wide_parts = grad_up_out(me1, low1, gpre, context, gattn)
    if split:
        down = reduce_part(*down_parts)
        wide = reduce_part(*[v.reshape(fsdp, rows_d, -1) for v in wide_parts])
    grads = ()
    for i in range(PARTS):
        grads = attend_back(qkv, context, gctx, lse, seg_col, seg_row, i * per, per, grads)
    dq, dk, dv, bias_sums = grads
    qkv_parts = grad_qkv(me1, x, dq, dk, dv, sums, up_sums, bias_sums, fsdp)
    if split:
        qkv_sum = reduce_part(*qkv_parts)
    dx = grad_in(me1, dq, dk, dv, res1, weight1)
    grad_input = deliver(dx)

    if split:
        both = lambda pair, axis: join(pair[0], pair[1], axis).astype(F32)
        grad_down_w = both(down, 0)
        w1 = D // 2
        grad_out = both([v[:, :w1] for v in wide], 1)
        grad_up = both([v[:, w1:] for v in wide], 1)
        grad_q = both([v[:rows_d] for v in qkv_sum], 1)
        tail = qkv_sum[0][rows_d:].astype(F32)
        g2, b2, db, g1, b1, ob, qb, vb = [tail[i, :rows_d] for i in range(8)]
        ub = tail[8, :rows_f]
    else:
        grad_down_w = scatter(join(*down_parts[::-1], 1).reshape(FF, D).astype(F32))
        wide = scatter(join(*wide_parts[::-1], 1).astype(F32))
        w1, w2 = D // 2, FF // 2
        grad_out = jnp.concatenate([wide[:, :w1], wide[:, w1 + w2 : 2 * w1 + w2]], 1)
        grad_up = jnp.concatenate([wide[:, w1 : w1 + w2], wide[:, 2 * w1 + w2 :]], 1)
        grad_q = scatter(join(*[v[:, :rows_d] for v in qkv_parts[::-1]], 2).reshape(D, 3 * D).astype(F32))
        by_dest = jnp.concatenate([sums[:6], bias_sums[:2]], 0).reshape(8, fsdp, rows_d)
        by_dest = by_dest.transpose(1, 0, 2).reshape(fsdp, 8 * rows_d)
        extra = jnp.concatenate([by_dest, up_sums[0].reshape(fsdp, rows_f)], 1)
        tail = scatter(extra).reshape(-1)
        g2, b2, db, g1, b1, ob, qb, vb = [tail[i * rows_d : (i + 1) * rows_d] for i in range(8)]
        ub = tail[8 * rows_d :]
    return (layer_out, grad_input, grad_q, qb, vb, grad_out, ob, g1, b1, grad_up, ub, grad_down_w,
            db, g2, b2)


PARTS = 3


def in_pieces(fsdp):
    return D // fsdp % 32 == 0 and FF // fsdp % 32 == 0


def solution(mesh):
    tok = P("fsdp", "sp", None)
    mat, vec = P("fsdp", None), P("fsdp")
    in_specs = (tok, mat, mat, vec, vec, mat, vec, vec, vec, mat, vec, mat, vec, vec, vec, tok)
    out_specs = (tok, tok, mat, vec, vec, mat, vec, vec, vec, mat, vec, mat, vec, vec, vec)

    return jax.shard_map(local, mesh=mesh, in_specs=in_specs, out_specs=out_specs, check_vma=False)
```

```python
import jax
import jax.numpy as jnp
from jax import lax
from jax.experimental import pallas as pl
from jax.experimental.pallas import tpu as pltpu
from jax.sharding import PartitionSpec as P


D = 768
H = 12
HD = 64
FF = 3072
SEQ = 1024
PAIRS = H // 2
EPS = 1e-05
MASKED = -1000000000.0
SCALE = HD ** (-0.5)
BF = jnp.bfloat16
F32 = jnp.float32
ROWS = 256
MIB = 1 << 20
SMALL = 16


ERFC = (
    0.2820844758103095,
    0.28240952292464144,
    0.24285408258103366,
    0.20367679547693512,
    -0.028968306758876145,
    0.2814702272328375,
    -0.49017537256556365,
    0.28601194065835034,
    -0.059363409284156475,
)


def nn(a, b):
    return lax.dot_general(a, b, (((1,), (0,)), ((), ())), preferred_element_type=F32)


def nt(a, b):
    return lax.dot_general(a, b, (((1,), (1,)), ((), ())), preferred_element_type=F32)


def tn(a, b):
    return lax.dot_general(a, b, (((0,), (0,)), ((), ())), preferred_element_type=F32)


def gelu_with_slope(x):
    z = jnp.abs(x) * 0.7071067811865476
    t = 1.0 / (1.0 + 0.5 * z)
    e = jnp.exp(-0.5 * (x * x))
    poly = jnp.full_like(t, 0.5 * ERFC[-1])
    for c in ERFC[-2::-1]:
        poly = poly * t + 0.5 * c
    tail = poly * t * e
    cdf = jnp.where(x >= 0, 1.0 - tail, tail)
    return x * cdf, cdf + x * (e * 0.3989422804014327)


def norm_rows(v):
    c = v - jnp.mean(v, -1, keepdims=True)
    r = lax.rsqrt(jnp.mean(c * c, -1, keepdims=True) + EPS)
    return c * r, r


def norm_rows_back(a, xhat, rstd):
    return rstd * (a - jnp.mean(a, -1, keepdims=True) - xhat * jnp.mean(a * xhat, -1, keepdims=True))


def piece_copies(pieces, by_rows, rows, cols, dst, sems, bits):
    core, x_bit, z_at = bits
    lo, nc = cols
    zs = len(pieces) // 4 if len(pieces[0].shape) == 2 else pieces[0].shape[0]
    copies = []
    for rc in range(2):
        row0 = rows * lax.bitwise_xor(core, rc) if by_rows else 0
        col0 = 0 if by_rows else pl.multiple_of(nc * lax.bitwise_xor(core, rc), nc)
        for rx in range(2):
            for z in range(zs):
                if len(pieces[0].shape) == 2:
                    src, at = pieces[(rc * 2 + rx) * zs + z], lax.bitwise_xor(z_at, z)
                else:
                    src, at = pieces[rc * 2 + rx].at[z], z
                row = row0 + rows * (2 if by_rows else 1) * (2 * at + lax.bitwise_xor(x_bit, rx))
                copies.append(
                    pltpu.make_async_copy(
                        src.at[pl.ds(0, rows), pl.ds(lo, nc)],
                        dst.at[pl.ds(pl.multiple_of(row, rows), rows), pl.ds(col0, nc)],
                        sems.at[(rc * 2 + rx) * zs + z],
                    )
                )
    return copies


def whole_copies(ref, cols, dst, sems):
    lo, nc = cols
    return [pltpu.make_async_copy(ref.at[:, pl.ds(lo, nc)], dst, sems.at[0])]


def weight_copies(weight, refs, rows, cols, full_cols, dst, sems, bits):
    kind = weight[0]
    if kind == "whole":
        return whole_copies(refs[0], full_cols, dst, sems)
    return piece_copies(refs, kind == "rows", rows, full_cols if kind == "rows" else cols, dst, sems, bits)


def copy_count(weight):
    kind, refs = weight
    if kind == "whole":
        return 1
    return len(refs) if len(refs[0].shape) == 2 else 4 * refs[0].shape[0]


def put_block(refs, step, value):
    for r, ref in enumerate(refs):
        @pl.when(step == r)
        def _():
            ref[...] = value


def start_all(copies):
    for c in copies:
        c.start()


def wait_all(copies):
    for c in copies:
        c.wait()


ANY = pl.BlockSpec(memory_space=pl.ANY)


def cost(us):
    return pl.CostEstimate(flops=int(us * 1e9), bytes_accessed=1 << 20, transcendentals=0)


def params(vmem=58):
    return pltpu.CompilerParams(
        dimension_semantics=("arbitrary",), vmem_limit_bytes=vmem * MIB
    )


def bits_of(me_ref):
    return lax.bitwise_and(me_ref[0], 1), me_ref[1], me_ref[2]


def pack(me, w, vectors):
    rows, width = w.shape[0], w.shape[1] // 2

    def kernel(me_ref, w_ref, *rest):
        v_refs, o_ref = rest[:-1], rest[-1]
        o_ref[:rows, :] = w_ref[...]
        o_ref[rows:, :] = jnp.zeros((SMALL, width), BF)
        for i, v in enumerate(v_refs):
            o_ref[rows + i : rows + i + 1, : v.shape[0]] = v[...].reshape(1, -1)

    one = lambda v: pl.BlockSpec(v.shape, lambda i, me: (0,))
    return pl.pallas_call(
        kernel,
        grid_spec=pltpu.PrefetchScalarGridSpec(
            num_scalar_prefetch=1,
            grid=(1,),
            in_specs=[pl.BlockSpec((rows, width), lambda i, me: (0, lax.bitwise_and(me[0], 1)))]
            + [one(v) for v in vectors],
            out_specs=pl.BlockSpec((rows + SMALL, width), lambda i, me: (0, 0)),
        ),
        out_shape=jax.ShapeDtypeStruct((rows + SMALL, width), BF),
        compiler_params=params(),
        cost_estimate=cost(2),
        name="pack",
    )(me, w, *vectors)


def block_at(r):
    return pl.BlockSpec((None, ROWS, D), lambda i, me: (lax.bitwise_xor(me[0], r), 0, 0))


WHOLE = pl.BlockSpec((ROWS, D), lambda i, me: (0, 0))


def deal(me, v):
    away = v.shape[0] - 1

    def kernel(me_ref, *refs):
        for r in range(away):
            refs[away + r][...] = refs[r][...]

    return pl.pallas_call(
        kernel,
        grid_spec=pltpu.PrefetchScalarGridSpec(
            num_scalar_prefetch=1, grid=(1,),
            in_specs=[block_at(r + 1) for r in range(away)],
            out_specs=[WHOLE] * away),
        out_shape=[jax.ShapeDtypeStruct((ROWS, D), v.dtype)] * away,
        compiler_params=params(),
        cost_estimate=cost(2),
        name="deal",
    )(me, *([v] * away))


def place(me, parts):
    n = len(parts)

    def kernel(me_ref, *refs):
        for r in range(n):
            @pl.when(pl.program_id(0) == r)
            def _():
                refs[n][...] = refs[r][...]

    return pl.pallas_call(
        kernel,
        grid_spec=pltpu.PrefetchScalarGridSpec(
            num_scalar_prefetch=1, grid=(n,),
            in_specs=[WHOLE] * n,
            out_specs=pl.BlockSpec((None, ROWS, D), lambda i, me: (lax.bitwise_xor(me[0], i), 0, 0))),
        out_shape=jax.ShapeDtypeStruct((n, ROWS, D), parts[0].dtype),
        compiler_params=params(),
        cost_estimate=cost(2),
        name="place",
    )(me, *parts)


def own_and_near(v, parts):
    return [v] + list(parts), [block_at(0)] + [WHOLE] * len(parts)


def get_block(refs, step, into):
    for r, ref in enumerate(refs):
        @pl.when(step == r)
        def _():
            into[...] = ref[...]


def project(me, x_own, x_near, weight, table, fsdp):
    _, refs = weight
    n = 3 * D
    count = copy_count(weight)
    per, per_up = D // fsdp, FF // fsdp
    x_args, x_specs = own_and_near(x_own, x_near)
    blocks = len(x_args)
    given = [] if table is None else list(table)

    def kernel(me_ref, *rest):
        x_refs, t_refs, w_refs = rest[:blocks], rest[blocks : blocks + len(given)], rest[blocks + len(given) : -8]
        o_ref, x_ref, tab_ref, up_ref, w_ref, sm_ref, sems, ssems = rest[-8:]
        get_block(x_refs, pl.program_id(0), x_ref)

        @pl.when(pl.program_id(0) == 0)
        def _():
            bits = bits_of(me_ref)
            copies = weight_copies(weight, w_refs, per, (0, n // 2), (0, n), w_ref, sems, bits)
            start_all(copies)
            if given:
                tab_ref[...] = t_refs[0][...]
                up_ref[...] = t_refs[1][...]
            else:
                zs = fsdp // 2
                vector_rows = [pltpu.make_async_copy(
                    w_refs[rx * zs + z].at[pl.ds(per, SMALL), pl.ds(0, per_up)],
                    sm_ref.at[2 * lax.bitwise_xor(bits[2], z) + lax.bitwise_xor(bits[1], rx)],
                    ssems.at[rx * zs + z]) for rx in range(2) for z in range(zs)]
                start_all(vector_rows)
                wait_all(vector_rows)
                for d in range(fsdp):
                    tab_ref[:, d * per : (d + 1) * per] = sm_ref[d, 0:8, :per].astype(F32)
                    up_ref[:, d * per_up : (d + 1) * per_up] = sm_ref[d, 8:16, :].astype(F32)
            wait_all(copies)

        xv = x_ref[...]
        o_ref[:, :D] = (nn(xv, w_ref[:, :D]) + tab_ref[6:7, :]).astype(BF)
        o_ref[:, D : 2 * D] = nn(xv, w_ref[:, D : 2 * D]).astype(BF)
        o_ref[:, 2 * D :] = (nn(xv, w_ref[:, 2 * D :]) + tab_ref[7:8, :]).astype(BF)

    rows = ROWS * blocks
    full = lambda s: pl.BlockSpec(s, lambda i, me: (0, 0))
    sd = jax.ShapeDtypeStruct
    return pl.pallas_call(
        kernel,
        grid_spec=pltpu.PrefetchScalarGridSpec(
            num_scalar_prefetch=1,
            grid=(blocks,),
            in_specs=x_specs + [full((8, D)), full((8, FF))][: len(given)] + [ANY] * len(refs),
            out_specs=[pl.BlockSpec((ROWS, n), lambda i, me: (i, 0)),
                       pl.BlockSpec((ROWS, D), lambda i, me: (i, 0)), full((8, D)), full((8, FF))],
            scratch_shapes=[pltpu.VMEM((D, n), BF), pltpu.VMEM((fsdp, SMALL, per_up), BF),
                            pltpu.SemaphoreType.DMA((count,)), pltpu.SemaphoreType.DMA((fsdp,))],
        ),
        out_shape=[sd((rows, n), BF), sd((rows, D), BF), sd((8, D), F32), sd((8, FF), F32)],
        compiler_params=params(),
        cost_estimate=cost(9),
        name="project",
    )(me, *x_args, *given, *refs)


def attend(qkv, seg_col, seg_row, first, count, before):
    chunk = 256

    def kernel(q_ref, k_ref, v_ref, sc_ref, sr_ref, *rest):
        o_ref, lse_ref = rest[-2:]
        lane = lax.broadcasted_iota(jnp.int32, (1, 2 * HD), 1)
        k = k_ref[...]
        vt = v_ref[...].T
        seg_k = sc_ref[...]

        for c in range(SEQ // chunk):
            at = pl.ds(c * chunk, chunk)
            q = q_ref[at, :] * jnp.asarray(SCALE, BF)
            same = seg_k == sr_ref[:, at]
            outs = []
            for h in range(2):
                mine = (lane < HD) if h == 0 else (lane >= HD)
                s = nt(k, jnp.where(mine, q, jnp.zeros_like(q)))
                s = jnp.where(same, s, MASKED)
                m = jnp.max(s, 0, keepdims=True)
                p = jnp.exp(s - m)
                l = jnp.sum(p, 0, keepdims=True)
                lse_ref[0, h : h + 1, at] = m + jnp.log(l)
                o = nn(vt, p.astype(BF))
                outs.append(o[h * HD : (h + 1) * HD] * (1.0 / l))
            o_ref[at, :] = jnp.concatenate(outs, 0).T.astype(BF)

    spec = lambda off: pl.BlockSpec((SEQ, 2 * HD), lambda i: (0, i + off + first))
    full = lambda s: pl.BlockSpec(s, lambda i: (0,) * len(s))
    return pl.pallas_call(
        kernel,
        grid=(count,),
        in_specs=[spec(0), spec(PAIRS), spec(2 * PAIRS), full((SEQ, 1)), full((1, SEQ))]
        + [ANY] * len(before),
        out_specs=[spec(0), pl.BlockSpec((1, 8, SEQ), lambda i: (i + first, 0, 0))],
        input_output_aliases={5 + i: i for i in range(len(before))},
        out_shape=[
            jax.ShapeDtypeStruct((SEQ, D), BF),
            jax.ShapeDtypeStruct((PAIRS, 8, SEQ), F32),
        ],
        compiler_params=params(),
        cost_estimate=cost(6 * count),
        name="attend",
    )(qkv, qkv, qkv, seg_col, seg_row, *before)


def attend_back(qkv, context, grad_context, lse, seg_col, seg_row, start, count, before):
    chunk = 256

    def kernel(q_ref, k_ref, v_ref, o_ref, g_ref, lse_ref, sc_ref, sr_ref, *rest):
        dq_ref, dk_ref, dv_ref, sum_ref, acc_ref, kt_ref = rest[-6:]
        lane = lax.broadcasted_iota(jnp.int32, (1, 2 * HD), 1)
        first = lane < HD
        q = q_ref[...] * jnp.asarray(SCALE, BF)
        g = g_ref[...]
        zero = jnp.zeros_like(q)
        prod = (g.astype(F32) * o_ref[...].astype(F32)).T
        inner = [jnp.sum(prod[h * HD : (h + 1) * HD], 0, keepdims=True) for h in range(2)]
        qm = [jnp.where(first, q, zero), jnp.where(first, zero, q)]
        gm = [jnp.where(first, g, zero), jnp.where(first, zero, g)]
        seg_q = sr_ref[...]
        kt_ref[...] = k_ref[...].T
        acc_ref[...] = jnp.zeros_like(acc_ref)
        sum_ref[1:2, :] = jnp.zeros((1, 2 * HD), F32)

        for c in range(SEQ // chunk):
            at = pl.ds(c * chunk, chunk)
            k = k_ref[at, :]
            v = v_ref[at, :]
            same = sc_ref[at, :] == seg_q
            dks, dvs = [], []
            for h in range(2):
                s = jnp.where(same, nt(k, qm[h]), MASKED)
                p = jnp.exp(s - lse_ref[0, h : h + 1, :])
                ds = (p * (nt(v, gm[h]) - inner[h])).astype(BF)
                dvs.append(nn(p.astype(BF), g))
                dks.append(nn(ds, q))
                half = pl.ds(h * HD, HD)
                acc_ref[half, :] += nn(kt_ref[half, at], ds)
            dk_ref[at, :] = jnp.where(first, dks[0], dks[1]).astype(BF)
            dv = jnp.where(first, dvs[0], dvs[1]).astype(BF)
            dv_ref[at, :] = dv
            sum_ref[1:2, :] += jnp.sum(dv.astype(F32), 0, keepdims=True)

        dq = (acc_ref[...].T * SCALE).astype(BF)
        dq_ref[...] = dq
        sum_ref[0:1, :] = jnp.sum(dq.astype(F32), 0, keepdims=True)

    spec = lambda off: pl.BlockSpec((SEQ, 2 * HD), lambda i: (0, i + off + start))
    full = lambda s: pl.BlockSpec(s, lambda i: (0,) * len(s))
    return pl.pallas_call(
        kernel,
        grid=(count,),
        in_specs=[spec(0), spec(PAIRS), spec(2 * PAIRS), spec(0), spec(0),
                  pl.BlockSpec((1, 8, SEQ), lambda i: (i + start, 0, 0)), full((SEQ, 1)),
                  full((1, SEQ))] + [ANY] * len(before),
        out_specs=[spec(0), spec(0), spec(0), pl.BlockSpec((8, 2 * HD), lambda i: (0, i + start))],
        input_output_aliases={8 + i: i for i in range(len(before))},
        out_shape=[jax.ShapeDtypeStruct((SEQ, D), BF)] * 3 + [jax.ShapeDtypeStruct((8, D), F32)],
        scratch_shapes=[pltpu.VMEM((2 * HD, SEQ), F32), pltpu.VMEM((2 * HD, SEQ), BF)],
        compiler_params=params(),
        cost_estimate=cost(6 * count),
        name="attend_back",
    )(qkv, qkv, qkv, context, grad_context, lse, seg_col, seg_row, *before)


def middle(me, context, x, g_own, g_near, vectors, up_bias, weight2, weight3, fsdp):
    _, refs2 = weight2
    _, refs3 = weight3
    count = copy_count(weight2)
    blocks = x.shape[0] // ROWS

    g_args, g_specs = own_and_near(g_own, g_near)

    def kernel(me_ref, c_ref, x_ref, vec_ref, ub_ref, *rest):
        g_refs, rest = rest[:blocks], rest[blocks:]
        w2, w3 = rest[: len(refs2)], rest[len(refs2) : len(refs2) + len(refs3)]
        o_refs = rest[len(refs2) + len(refs3) :][:blocks]
        (act_ref, gpre_ref, n1_ref, gffn_ref, gattn_ref, gres_ref, gctx_ref,
         sum_ref, usum_ref, wo, wu, wd, slope, g_ref, s_o, s_u, s_d) = rest[len(refs2) + len(refs3) + blocks :]
        step = pl.program_id(0)
        get_block(g_refs, step, g_ref)
        bits = bits_of(me_ref)
        co = weight_copies(weight2, w2, D // fsdp, (0, D // 2), (0, D), wo, s_o, bits)
        cu = weight_copies(weight2, w2, D // fsdp, (D // 2, FF // 2), (D, FF), wu, s_u, bits)
        cd = weight_copies(weight3, w3, FF // fsdp // 2, None, (0, D), wd, s_d, bits)

        @pl.when(step == 0)
        def _():
            start_all(co)
            start_all(cu)
            start_all(cd)
            sum_ref[...] = jnp.zeros_like(sum_ref)
            usum_ref[...] = jnp.zeros_like(usum_ref)
            wait_all(co)

        out_bias, gain1, shift1 = vec_ref[0:1], vec_ref[1:2], vec_ref[2:3]
        down_bias, gain2, shift2 = vec_ref[3:4], vec_ref[4:5], vec_ref[5:6]
        attn = nn(c_ref[...], wo[...]) + out_bias
        xhat1, rstd1 = norm_rows(x_ref[...].astype(F32) + attn)
        normed1 = xhat1 * gain1 + shift1
        low1 = normed1.astype(BF)
        n1_ref[...] = low1

        @pl.when(step == 0)
        def _():
            wait_all(cu)
            wait_all(cd)

        ffn = jnp.zeros((ROWS, D), F32)
        for lo in range(0, FF, D):
            at = slice(lo, lo + D)
            pre = nn(low1, wu[:, at]) + ub_ref[0:1, at]
            act, sl = gelu_with_slope(pre)
            act = act.astype(BF)
            act_ref[:, at] = act
            slope[:, at] = sl
            ffn = ffn + nn(act, wd[at, :])
        xhat2, rstd2 = norm_rows(normed1 + (ffn + down_bias))
        out = (xhat2 * gain2 + shift2).astype(BF)
        put_block(o_refs, step, out)
        gr = g_ref[...].astype(F32)
        res2 = norm_rows_back(gr * gain2, xhat2, rstd2)
        gffn = res2.astype(BF)
        gffn_ref[...] = gffn
        rs = lambda v: jnp.sum(v, 0, keepdims=True)
        sum_ref[0:1] += rs(gr * xhat2)
        sum_ref[1:2] += rs(gr)
        sum_ref[2:3] += rs(gffn.astype(F32))
        gn1 = res2
        for lo in range(0, FF, D):
            at = slice(lo, lo + D)
            gpre = (nt(gffn, wd[at, :]) * slope[:, at]).astype(BF)
            gpre_ref[:, at] = gpre
            usum_ref[0:1, at] += rs(gpre.astype(F32))
            gn1 = gn1 + nt(gpre, wu[:, at])
        sum_ref[3:4] += rs(gn1 * xhat1)
        sum_ref[4:5] += rs(gn1)
        res1 = norm_rows_back(gn1 * gain1, xhat1, rstd1)
        gres_ref[...] = res1
        gattn = res1.astype(BF)
        gattn_ref[...] = gattn
        sum_ref[5:6] += rs(gattn.astype(F32))
        gctx_ref[...] = nt(gattn, wo[...]).astype(BF)

    rows = x.shape[0]
    blk = lambda n: pl.BlockSpec((ROWS, n), lambda i, me: (i, 0))
    full = lambda s: pl.BlockSpec(s, lambda i, me: (0,) * len(s))
    sd = jax.ShapeDtypeStruct
    return pl.pallas_call(
        kernel,
        grid_spec=pltpu.PrefetchScalarGridSpec(
            num_scalar_prefetch=1,
            grid=(rows // ROWS,),
            in_specs=[blk(D), blk(D), full((8, D)), full((8, FF))] + g_specs
            + [ANY] * (len(refs2) + len(refs3)),
            out_specs=[full((ROWS, D))] * blocks + [blk(FF), blk(FF), blk(D), blk(D), blk(D), blk(D), blk(D),
                       full((8, D)), full((8, FF))],
            scratch_shapes=[
                pltpu.VMEM((D, D), BF), pltpu.VMEM((D, FF), BF), pltpu.VMEM((FF, D), BF),
                pltpu.VMEM((ROWS, FF), F32), pltpu.VMEM((ROWS, D), BF),
                pltpu.SemaphoreType.DMA((count,)), pltpu.SemaphoreType.DMA((count,)),
                pltpu.SemaphoreType.DMA((count,)),
            ],
        ),
        out_shape=[sd((ROWS, D), BF)] * blocks + [sd((rows, FF), BF), sd((rows, FF), BF), sd((rows, D), BF),
                   sd((rows, D), BF), sd((rows, D), BF), sd((rows, D), F32), sd((rows, D), BF),
                   sd((8, D), F32), sd((8, FF), F32)],
        compiler_params=params(),
        cost_estimate=cost(48),
        name="middle",
    )(me, context, x, vectors, up_bias, *g_args, *refs2, *refs3)


def grad_down(me, act, grad_ffn, fsdp):
    per = FF // fsdp
    steps = 8
    width = FF // steps
    inner = width // per

    def kernel(me_ref, a_ref, g_ref, send_ref, keep_ref, acc_ref):
        core, _, _ = bits_of(me_ref)
        acc_ref[...] = tn(a_ref[...], g_ref[...])
        n = per // 2
        for i in range(inner):
            take = lambda b: acc_ref[pl.ds(pl.multiple_of(i * per + n * b, n), n), :].astype(BF)
            send_ref[i] = take(1 - core)
            keep_ref[i] = take(core)

    rows = act.shape[0]
    out = jax.ShapeDtypeStruct((fsdp, per // 2, D), BF)
    ospec = pl.BlockSpec((inner, per // 2, D), lambda i, me: (i, 0, 0))
    return pl.pallas_call(
        kernel,
        grid_spec=pltpu.PrefetchScalarGridSpec(
            num_scalar_prefetch=1,
            grid=(steps,),
            in_specs=[pl.BlockSpec((rows, width), lambda i, me: (0, i)),
                      pl.BlockSpec((rows, D), lambda i, me: (0, 0))],
            out_specs=[ospec, ospec],
            scratch_shapes=[pltpu.VMEM((width, D), F32)],
        ),
        out_shape=[out, out],
        compiler_params=params(),
        cost_estimate=cost(12),
        name="grad_down",
    )(me, act, grad_ffn)


def write_half(step, slots, send_ref, keep_ref, sems):
    sending = pltpu.make_async_copy(slots.at[0], send_ref, sems.at[0])
    keeping = pltpu.make_async_copy(slots.at[1], keep_ref, sems.at[1])
    pl.when(step == 0)(sending.start)

    @pl.when(step == 1)
    def _():
        keeping.start()
        sending.wait()
        keeping.wait()


def half_of(i, core):
    return jnp.where(i == 0, 1 - core, core)


def grad_up_out(me, low1, grad_pre, context, grad_attn):
    wu, wo = FF // 2, D // 2

    def kernel(me_ref, l_ref, p_ref, c_ref, a_ref, send_ref, keep_ref, slots, sems):
        step = pl.program_id(0)
        slots[step, :, :wo] = tn(c_ref[...], a_ref[...]).astype(BF)
        low = l_ref[...]
        for lo in range(0, wu, D):
            slots[step, :, wo + lo : wo + lo + D] = tn(low, p_ref[:, lo : lo + D]).astype(BF)
        write_half(step, slots, send_ref, keep_ref, sems)

    rows = low1.shape[0]
    half = lambda n: pl.BlockSpec(
        (rows, n), lambda i, me: (0, half_of(i, lax.bitwise_and(me[0], 1))))
    full = pl.BlockSpec((rows, D), lambda i, me: (0, 0))
    return pl.pallas_call(
        kernel,
        grid_spec=pltpu.PrefetchScalarGridSpec(
            num_scalar_prefetch=1, grid=(2,),
            in_specs=[full, half(wu), full, half(wo)], out_specs=[ANY] * 2,
            scratch_shapes=[pltpu.VMEM((2, D, wu + wo), BF), pltpu.SemaphoreType.DMA((2,))]),
        out_shape=[jax.ShapeDtypeStruct((D, wu + wo), BF)] * 2,
        compiler_params=params(),
        cost_estimate=cost(12),
        name="grad_up_out",
    )(me, low1, grad_pre, context, grad_attn)


def grad_qkv(me, x, dq, dk, dv, sums, up_sums, bias_sums, fsdp):
    w = 3 * D // 2
    per, per_up = D // fsdp, FF // fsdp
    tall = per + SMALL

    def kernel(me_ref, x_ref, q_ref, k_ref, v_ref, s_ref, u_ref, b_ref, send_ref, keep_ref, slots, sems):
        core, _, _ = bits_of(me_ref)
        step = pl.program_id(0)
        b = half_of(step, core)

        def put(lo, val):
            val = val.astype(BF)
            for d in range(fsdp):
                slots[step, d, :per, lo : lo + val.shape[1]] = val[d * per : (d + 1) * per]

        @pl.when(b == 0)
        def _():
            put(0, tn(x_ref[...], q_ref[...]))
            put(D, tn(x_ref[...], k_ref[:, : D // 2]))

        @pl.when(b == 1)
        def _():
            put(0, tn(x_ref[...], k_ref[:, D // 2 :]))
            put(D // 2, tn(x_ref[...], v_ref[...]))

        rows = jnp.concatenate([s_ref[0:6], b_ref[0:2]], 0)
        for d in range(fsdp):
            slots[step, d, per:, :] = jnp.zeros((SMALL, w), BF)
            slots[step, d, per : per + 8, :per] = rows[:, d * per : (d + 1) * per].astype(BF)
            slots[step, d, per + 8 : per + 9, :per_up] = u_ref[0:1, d * per_up : (d + 1) * per_up].astype(BF)
        write_half(step, slots, send_ref, keep_ref, sems)

    rows = x.shape[0]
    full = lambda s: pl.BlockSpec(s, lambda i, me: (0, 0))
    return pl.pallas_call(
        kernel,
        grid_spec=pltpu.PrefetchScalarGridSpec(
            num_scalar_prefetch=1, grid=(2,),
            in_specs=[full((rows, D))] * 4 + [full((8, D)), full((8, FF)), full((8, D))],
            out_specs=[ANY] * 2,
            scratch_shapes=[pltpu.VMEM((2, fsdp, tall, w), BF), pltpu.SemaphoreType.DMA((2,))]),
        out_shape=[jax.ShapeDtypeStruct((fsdp, tall, w), BF)] * 2,
        compiler_params=params(),
        cost_estimate=cost(9),
        name="grad_qkv",
    )(me, x, dq, dk, dv, sums, up_sums, bias_sums)


def grad_in(me, dq, dk, dv, res1, weight, fsdp):
    _, refs = weight
    n = 3 * D
    count = copy_count(weight)

    def kernel(me_ref, q_ref, k_ref, v_ref, r_ref, *rest):
        w_refs, o_refs, (w_ref, sems) = rest[: len(refs)], rest[len(refs) : -2], rest[-2:]

        @pl.when(pl.program_id(0) == 0)
        def _():
            copies = weight_copies(weight, w_refs, D // fsdp, (0, n // 2), (0, n), w_ref, sems, bits_of(me_ref))
            start_all(copies)
            wait_all(copies)

        total = r_ref[...] + nt(q_ref[...], w_ref[:, :D])
        total = total + nt(k_ref[...], w_ref[:, D : 2 * D])
        total = total + nt(v_ref[...], w_ref[:, 2 * D :])
        put_block(o_refs, pl.program_id(0), total.astype(BF))

    rows = dq.shape[0]
    blocks = rows // ROWS
    blk = pl.BlockSpec((ROWS, D), lambda i, me: (i, 0))
    return pl.pallas_call(
        kernel,
        grid_spec=pltpu.PrefetchScalarGridSpec(
            num_scalar_prefetch=1, grid=(rows // ROWS,),
            in_specs=[blk] * 4 + [ANY] * len(refs),
            out_specs=[pl.BlockSpec((ROWS, D), lambda i, me: (0, 0))] * blocks,
            scratch_shapes=[pltpu.VMEM((D, n), BF), pltpu.SemaphoreType.DMA((count,))]),
        out_shape=[jax.ShapeDtypeStruct((ROWS, D), BF)] * blocks,
        compiler_params=params(),
        cost_estimate=cost(9),
        name="grad_in",
    )(me, dq, dk, dv, res1, *refs)


def local(hidden_in, doc_starts, w_qkv, query_bias, value_bias, w_out, out_bias, norm1_gain,
          norm1_bias, w_up, up_bias, w_down, down_bias, norm2_gain, norm2_bias, cotangent):
    fsdp, sp = lax.axis_size("fsdp"), lax.axis_size("sp")
    seqs, span, _ = hidden_in.shape
    assert sp == 4 and seqs == sp and span * sp == SEQ and span == ROWS
    me = lax.axis_index("sp").astype(jnp.int32)
    core = me & 1
    row = lax.axis_index("fsdp").astype(jnp.int32)
    xb, zs = row & 1, fsdp // 2
    me1 = jnp.stack([me, xb, row >> 1])
    high = me >> 1
    rows_d, rows_f = D // fsdp, FF // fsdp
    split = in_pieces(fsdp)

    def partner(v, bit):
        return lax.ppermute(v, "sp", [(i, i ^ bit) for i in range(sp)])

    def away(v, bits):
        return lax.ppermute(v, "fsdp", [(i, i ^ bits) for i in range(fsdp)])

    def across(v):
        return away(v, 1)

    lines = [[2 * z + b for z in range(zs)] for b in range(2)]

    def along(v):
        return lax.all_to_all(v, "fsdp", 0, 0, axis_index_groups=lines, tiled=True)

    def swap(parts):
        two, three, one = [partner(parts[r - 1], r) for r in (2, 3, 1)]
        return [one, two, three]

    def fetch(v):
        return swap(deal(me1, v))

    def deliver(parts):
        return place(me1, [parts[0]] + swap(parts[1:]))

    def each(v):
        return jnp.broadcast_to(v[None], (zs,) + v.shape)

    def half_cols(w):
        return lax.dynamic_slice(w, (0, core * (w.shape[1] // 2)), (w.shape[0], w.shape[1] // 2))

    def spread(v):
        a = along(each(v))
        b = across(a)
        return a, b, partner(a, 1), partner(b, 1)

    def spread_apart(v):
        line = [v] + [away(v, 2 * z) for z in range(1, zs)]
        line += [across(a) for a in line]
        return line + [partner(a, 1) for a in line]

    small = [out_bias, norm1_gain, norm1_bias, down_bias, norm2_gain, norm2_bias, query_bias,
             value_bias, up_bias]
    x_near = fetch(hidden_in)
    if split:
        weight1 = ("cols", spread_apart(pack(me1, w_qkv, small)))
        table = None
        weight2 = ("cols", spread(jnp.concatenate([half_cols(w_out), half_cols(w_up)], 1)))
        down = lax.dynamic_slice(w_down, (core * (rows_f // 2), 0), (rows_f // 2, D))
        weight3 = ("rows", spread(down))
    else:
        every = lax.all_gather(jnp.concatenate(small), "fsdp", axis=0).astype(F32)
        table = every[:, : 8 * rows_d].reshape(fsdp, 8, rows_d).transpose(1, 0, 2).reshape(8, D)
        full_up_bias = jnp.broadcast_to(every[:, 8 * rows_d :].reshape(1, FF), (8, FF))
        table = (table, full_up_bias)
        gather = lambda w: lax.all_gather(w, "fsdp", axis=0, tiled=True)
        weight1 = ("whole", (gather(w_qkv),))
        weight2 = ("whole", (gather(jnp.concatenate([w_out, w_up], 1)),))
        weight3 = ("whole", (gather(w_down),))
    g_near = fetch(cotangent)

    starts = lax.dynamic_slice(doc_starts, (me, 0), (1, doc_starts.shape[1]))
    order = jnp.arange(SEQ, dtype=jnp.int32)
    position = ((order // span) ^ me) * span + order % span
    seg = jnp.sum((position[:, None] >= starts).astype(jnp.int32), -1)
    seg_col, seg_row = seg[:, None], seg[None, :]

    qkv, x, table, full_up_bias = project(me1, hidden_in, x_near, weight1, table, fsdp)
    context = ()
    per = PAIRS // PARTS
    for i in range(PARTS):
        context = attend(qkv, seg_col, seg_row, i * per, per, context)
    context, lse = context
    (*out, act, gpre, low1, gffn, gattn, res1, gctx, sums, up_sums) = middle(
        me1, context, x, cotangent, g_near, table, full_up_bias, weight2, weight3, fsdp)
    layer_out = deliver(out)

    def add(a, b):
        return (a.astype(F32) + b.astype(F32)).astype(BF)

    def join(mine, other, axis, bit=core):
        return jnp.where(bit == 0, jnp.concatenate([mine, other], axis),
                         jnp.concatenate([other, mine], axis))

    def pick(v, bit):
        return lax.dynamic_index_in_dim(v, bit, 1, False)

    def over_rows(v):
        v = v.reshape((zs, 2) + v.shape[1:])
        v = add(pick(v, xb), across(pick(v, 1 - xb)))
        return jnp.sum(along(v).astype(F32), 0).astype(BF)

    def reduce_part(send, keep):
        total = over_rows(add(keep, partner(send, 1)))
        total = add(total, partner(total, 2))
        return total, partner(total, 1)

    def reduce_by_high(send, keep):
        v = add(keep, partner(send, 1))
        v = v.reshape(fsdp, 2, v.shape[1] // 2, v.shape[2])
        v = add(pick(v, high), partner(pick(v, 1 - high), 2))
        total = over_rows(v)
        total = join(total, partner(total, 2), 0, high)
        return total, partner(total, 1)

    def scatter(v):
        part = lax.psum_scatter(v, "fsdp", scatter_dimension=0, tiled=True)
        return lax.psum(part, "sp").astype(F32)

    down_parts = grad_down(me1, act, gffn, fsdp)
    wide_parts = grad_up_out(me1, low1, gpre, context, gattn)
    if split:
        down = reduce_part(*down_parts)
        wide = reduce_by_high(*[v.reshape(fsdp, rows_d, -1) for v in wide_parts])
    grads = ()
    for i in range(PARTS):
        grads = attend_back(qkv, context, gctx, lse, seg_col, seg_row, i * per, per, grads)
    dq, dk, dv, bias_sums = grads
    qkv_parts = grad_qkv(me1, x, dq, dk, dv, sums, up_sums, bias_sums, fsdp)
    if split:
        qkv_sum = reduce_part(*qkv_parts)
    dx = grad_in(me1, dq, dk, dv, res1, weight1, fsdp)
    grad_input = deliver(dx)

    if split:
        both = lambda pair, axis: join(pair[0], pair[1], axis).astype(F32)
        grad_down_w = both(down, 0)
        w1 = D // 2
        grad_out = both([v[:, :w1] for v in wide], 1)
        grad_up = both([v[:, w1:] for v in wide], 1)
        grad_q = both([v[:rows_d] for v in qkv_sum], 1)
        tail = qkv_sum[0][rows_d:].astype(F32)
        g2, b2, db, g1, b1, ob, qb, vb = [tail[i, :rows_d] for i in range(8)]
        ub = tail[8, :rows_f]
    else:
        grad_down_w = scatter(join(*down_parts[::-1], 1).reshape(FF, D).astype(F32))
        wide = scatter(join(*wide_parts[::-1], 1).astype(F32))
        w1, w2 = D // 2, FF // 2
        grad_out = jnp.concatenate([wide[:, :w1], wide[:, w1 + w2 : 2 * w1 + w2]], 1)
        grad_up = jnp.concatenate([wide[:, w1 : w1 + w2], wide[:, 2 * w1 + w2 :]], 1)
        grad_q = scatter(join(*[v[:, :rows_d] for v in qkv_parts[::-1]], 2).reshape(D, 3 * D).astype(F32))
        by_dest = jnp.concatenate([sums[:6], bias_sums[:2]], 0).reshape(8, fsdp, rows_d)
        by_dest = by_dest.transpose(1, 0, 2).reshape(fsdp, 8 * rows_d)
        extra = jnp.concatenate([by_dest, up_sums[0].reshape(fsdp, rows_f)], 1)
        tail = scatter(extra).reshape(-1)
        g2, b2, db, g1, b1, ob, qb, vb = [tail[i * rows_d : (i + 1) * rows_d] for i in range(8)]
        ub = tail[8 * rows_d :]
    return (layer_out, grad_input, grad_q, qb, vb, grad_out, ob, g1, b1, grad_up, ub, grad_down_w,
            db, g2, b2)


PARTS = 3


def in_pieces(fsdp):
    return D // fsdp % 32 == 0 and FF // fsdp % 32 == 0


def solution(mesh):
    tok = P("fsdp", "sp", None)
    mat, vec = P("fsdp", None), P("fsdp")
    in_specs = (tok, mat, mat, vec, vec, mat, vec, vec, vec, mat, vec, mat, vec, vec, vec, tok)
    out_specs = (tok, tok, mat, vec, vec, mat, vec, vec, vec, mat, vec, mat, vec, vec, vec)

    return jax.shard_map(local, mesh=mesh, in_specs=in_specs, out_specs=out_specs, check_vma=False)
```

```python
import jax
import jax.numpy as jnp
from jax import lax
from jax.experimental import pallas as pl
from jax.experimental.pallas import tpu as pltpu
from jax.sharding import PartitionSpec as P


D = 768
H = 12
HD = 64
FF = 3072
SEQ = 1024
PAIRS = H // 2
EPS = 1e-05
MASKED = -1000000000.0
SCALE = HD ** (-0.5)
BF = jnp.bfloat16
F32 = jnp.float32
ROWS = 256
MIB = 1 << 20
SMALL = 16


ERFC = (
    0.2820844758103095,
    0.28240952292464144,
    0.24285408258103366,
    0.20367679547693512,
    -0.028968306758876145,
    0.2814702272328375,
    -0.49017537256556365,
    0.28601194065835034,
    -0.059363409284156475,
)


def nn(a, b):
    return lax.dot_general(a, b, (((1,), (0,)), ((), ())), preferred_element_type=F32)


def nt(a, b):
    return lax.dot_general(a, b, (((1,), (1,)), ((), ())), preferred_element_type=F32)


def tn(a, b):
    return lax.dot_general(a, b, (((0,), (0,)), ((), ())), preferred_element_type=F32)


def gelu_with_slope(x):
    z = jnp.abs(x) * 0.7071067811865476
    t = 1.0 / (1.0 + 0.5 * z)
    e = jnp.exp(-0.5 * (x * x))
    poly = jnp.full_like(t, 0.5 * ERFC[-1])
    for c in ERFC[-2::-1]:
        poly = poly * t + 0.5 * c
    tail = poly * t * e
    cdf = jnp.where(x >= 0, 1.0 - tail, tail)
    return x * cdf, cdf + x * (e * 0.3989422804014327)


def norm_rows(v):
    c = v - jnp.mean(v, -1, keepdims=True)
    r = lax.rsqrt(jnp.mean(c * c, -1, keepdims=True) + EPS)
    return c * r, r


def norm_rows_back(a, xhat, rstd):
    return rstd * (a - jnp.mean(a, -1, keepdims=True) - xhat * jnp.mean(a * xhat, -1, keepdims=True))


def piece_copies(pieces, by_rows, rows, cols, dst, sems, bits):
    core, x_bit, z_at = bits
    lo, nc = cols
    per = len(pieces) // 4
    copies = []
    for rc in range(2):
        row0 = rows * lax.bitwise_xor(core, rc) if by_rows else 0
        col0 = 0 if by_rows else pl.multiple_of(nc * lax.bitwise_xor(core, rc), nc)
        for rx in range(2):
            line = []
            for ref in pieces[(rc * 2 + rx) * per : (rc * 2 + rx + 1) * per]:
                line += [ref] if len(ref.shape) == 2 else [ref.at[i] for i in range(ref.shape[0])]
            for z, src in enumerate(line):
                at = 2 * lax.bitwise_xor(z_at, z) + lax.bitwise_xor(x_bit, rx)
                row = row0 + rows * (2 if by_rows else 1) * at
                copies.append(
                    pltpu.make_async_copy(
                        src.at[pl.ds(0, rows), pl.ds(lo, nc)],
                        dst.at[pl.ds(pl.multiple_of(row, rows), rows), pl.ds(col0, nc)],
                        sems.at[len(copies)],
                    )
                )
    return copies


def whole_copies(ref, cols, dst, sems):
    lo, nc = cols
    return [pltpu.make_async_copy(ref.at[:, pl.ds(lo, nc)], dst, sems.at[0])]


def weight_copies(weight, refs, rows, cols, full_cols, dst, sems, bits):
    kind = weight[0]
    if kind == "whole":
        return whole_copies(refs[0], full_cols, dst, sems)
    return piece_copies(refs, kind == "rows", rows, full_cols if kind == "rows" else cols, dst, sems, bits)


def copy_count(weight):
    kind, refs = weight
    if kind == "whole":
        return 1
    return sum(1 if len(v.shape) == 2 else v.shape[0] for v in refs)


def put_block(refs, step, value):
    for r, ref in enumerate(refs):
        @pl.when(step == r)
        def _():
            ref[...] = value


def start_all(copies):
    for c in copies:
        c.start()


def wait_all(copies):
    for c in copies:
        c.wait()


ANY = pl.BlockSpec(memory_space=pl.ANY)


def cost(us):
    return pl.CostEstimate(flops=int(us * 1e9), bytes_accessed=1 << 20, transcendentals=0)


def params(vmem=58):
    return pltpu.CompilerParams(
        dimension_semantics=("arbitrary",), vmem_limit_bytes=vmem * MIB
    )


def bits_of(me_ref):
    return lax.bitwise_and(me_ref[0], 1), me_ref[1], me_ref[2]


def pack(me, w, vectors):
    rows, width = w.shape[0], w.shape[1] // 2

    def kernel(me_ref, w_ref, *rest):
        v_refs, o_ref = rest[:-1], rest[-1]
        o_ref[:rows, :] = w_ref[...]
        o_ref[rows:, :] = jnp.zeros((SMALL, width), BF)
        for i, v in enumerate(v_refs):
            o_ref[rows + i : rows + i + 1, : v.shape[0]] = v[...].reshape(1, -1)

    one = lambda v: pl.BlockSpec(v.shape, lambda i, me: (0,))
    return pl.pallas_call(
        kernel,
        grid_spec=pltpu.PrefetchScalarGridSpec(
            num_scalar_prefetch=1,
            grid=(1,),
            in_specs=[pl.BlockSpec((rows, width), lambda i, me: (0, lax.bitwise_and(me[0], 1)))]
            + [one(v) for v in vectors],
            out_specs=pl.BlockSpec((rows + SMALL, width), lambda i, me: (0, 0)),
        ),
        out_shape=jax.ShapeDtypeStruct((rows + SMALL, width), BF),
        compiler_params=params(),
        cost_estimate=cost(2),
        name="pack",
    )(me, w, *vectors)


def block_at(r):
    return pl.BlockSpec((None, ROWS, D), lambda i, me: (lax.bitwise_xor(me[0], r), 0, 0))


WHOLE = pl.BlockSpec((ROWS, D), lambda i, me: (0, 0))


def deal(me, v):
    away = v.shape[0] - 1

    def kernel(me_ref, *refs):
        for r in range(away):
            refs[away + r][...] = refs[r][...]

    return pl.pallas_call(
        kernel,
        grid_spec=pltpu.PrefetchScalarGridSpec(
            num_scalar_prefetch=1, grid=(1,),
            in_specs=[block_at(r + 1) for r in range(away)],
            out_specs=[WHOLE] * away),
        out_shape=[jax.ShapeDtypeStruct((ROWS, D), v.dtype)] * away,
        compiler_params=params(),
        cost_estimate=cost(2),
        name="deal",
    )(me, *([v] * away))


def place(me, parts):
    n = len(parts)

    def kernel(me_ref, *refs):
        for r in range(n):
            @pl.when(pl.program_id(0) == r)
            def _():
                refs[n][...] = refs[r][...]

    return pl.pallas_call(
        kernel,
        grid_spec=pltpu.PrefetchScalarGridSpec(
            num_scalar_prefetch=1, grid=(n,),
            in_specs=[WHOLE] * n,
            out_specs=pl.BlockSpec((None, ROWS, D), lambda i, me: (lax.bitwise_xor(me[0], i), 0, 0))),
        out_shape=jax.ShapeDtypeStruct((n, ROWS, D), parts[0].dtype),
        compiler_params=params(),
        cost_estimate=cost(2),
        name="place",
    )(me, *parts)


def own_and_near(v, parts):
    return [v] + list(parts), [block_at(0)] + [WHOLE] * len(parts)


def get_block(refs, step, into):
    for r, ref in enumerate(refs):
        @pl.when(step == r)
        def _():
            into[...] = ref[...]


def project(me, x_own, x_near, weight, table, fsdp):
    _, refs = weight
    n = 3 * D
    count = copy_count(weight)
    per, per_up = D // fsdp, FF // fsdp
    x_args, x_specs = own_and_near(x_own, x_near)
    blocks = len(x_args)
    given = [] if table is None else list(table)

    def kernel(me_ref, *rest):
        x_refs, t_refs, w_refs = rest[:blocks], rest[blocks : blocks + len(given)], rest[blocks + len(given) : -8]
        o_ref, x_ref, tab_ref, up_ref, w_ref, sm_ref, sems, ssems = rest[-8:]
        get_block(x_refs, pl.program_id(0), x_ref)

        @pl.when(pl.program_id(0) == 0)
        def _():
            bits = bits_of(me_ref)
            copies = weight_copies(weight, w_refs, per, (0, n // 2), (0, n), w_ref, sems, bits)
            start_all(copies)
            if given:
                tab_ref[...] = t_refs[0][...]
                up_ref[...] = t_refs[1][...]
            else:
                zs = fsdp // 2
                vector_rows = [pltpu.make_async_copy(
                    w_refs[rx * zs + z].at[pl.ds(per, SMALL), pl.ds(0, per_up)],
                    sm_ref.at[2 * lax.bitwise_xor(bits[2], z) + lax.bitwise_xor(bits[1], rx)],
                    ssems.at[rx * zs + z]) for rx in range(2) for z in range(zs)]
                start_all(vector_rows)
                wait_all(vector_rows)
                for d in range(fsdp):
                    tab_ref[:, d * per : (d + 1) * per] = sm_ref[d, 0:8, :per].astype(F32)
                    up_ref[:, d * per_up : (d + 1) * per_up] = sm_ref[d, 8:16, :].astype(F32)
            wait_all(copies)

        xv = x_ref[...]
        o_ref[:, :D] = (nn(xv, w_ref[:, :D]) + tab_ref[6:7, :]).astype(BF)
        o_ref[:, D : 2 * D] = nn(xv, w_ref[:, D : 2 * D]).astype(BF)
        o_ref[:, 2 * D :] = (nn(xv, w_ref[:, 2 * D :]) + tab_ref[7:8, :]).astype(BF)

    rows = ROWS * blocks
    full = lambda s: pl.BlockSpec(s, lambda i, me: (0, 0))
    sd = jax.ShapeDtypeStruct
    return pl.pallas_call(
        kernel,
        grid_spec=pltpu.PrefetchScalarGridSpec(
            num_scalar_prefetch=1,
            grid=(blocks,),
            in_specs=x_specs + [full((8, D)), full((8, FF))][: len(given)] + [ANY] * len(refs),
            out_specs=[pl.BlockSpec((ROWS, n), lambda i, me: (i, 0)),
                       pl.BlockSpec((ROWS, D), lambda i, me: (i, 0)), full((8, D)), full((8, FF))],
            scratch_shapes=[pltpu.VMEM((D, n), BF), pltpu.VMEM((fsdp, SMALL, per_up), BF),
                            pltpu.SemaphoreType.DMA((count,)), pltpu.SemaphoreType.DMA((fsdp,))],
        ),
        out_shape=[sd((rows, n), BF), sd((rows, D), BF), sd((8, D), F32), sd((8, FF), F32)],
        compiler_params=params(),
        cost_estimate=cost(9),
        name="project",
    )(me, *x_args, *given, *refs)


def attend(qkv, seg_col, seg_row, first, count, before):
    chunk = 256

    def kernel(q_ref, k_ref, v_ref, sc_ref, sr_ref, *rest):
        o_ref, lse_ref = rest[-2:]
        lane = lax.broadcasted_iota(jnp.int32, (1, 2 * HD), 1)
        k = k_ref[...]
        vt = v_ref[...].T
        seg_k = sc_ref[...]

        for c in range(SEQ // chunk):
            at = pl.ds(c * chunk, chunk)
            q = q_ref[at, :] * jnp.asarray(SCALE, BF)
            same = seg_k == sr_ref[:, at]
            outs = []
            for h in range(2):
                mine = (lane < HD) if h == 0 else (lane >= HD)
                s = nt(k, jnp.where(mine, q, jnp.zeros_like(q)))
                s = jnp.where(same, s, MASKED)
                m = jnp.max(s, 0, keepdims=True)
                p = jnp.exp(s - m)
                l = jnp.sum(p, 0, keepdims=True)
                lse_ref[0, h : h + 1, at] = m + jnp.log(l)
                o = nn(vt, p.astype(BF))
                outs.append(o[h * HD : (h + 1) * HD] * (1.0 / l))
            o_ref[at, :] = jnp.concatenate(outs, 0).T.astype(BF)

    spec = lambda off: pl.BlockSpec((SEQ, 2 * HD), lambda i: (0, i + off + first))
    full = lambda s: pl.BlockSpec(s, lambda i: (0,) * len(s))
    return pl.pallas_call(
        kernel,
        grid=(count,),
        in_specs=[spec(0), spec(PAIRS), spec(2 * PAIRS), full((SEQ, 1)), full((1, SEQ))]
        + [ANY] * len(before),
        out_specs=[spec(0), pl.BlockSpec((1, 8, SEQ), lambda i: (i + first, 0, 0))],
        input_output_aliases={5 + i: i for i in range(len(before))},
        out_shape=[
            jax.ShapeDtypeStruct((SEQ, D), BF),
            jax.ShapeDtypeStruct((PAIRS, 8, SEQ), F32),
        ],
        compiler_params=params(),
        cost_estimate=cost(6 * count),
        name="attend",
    )(qkv, qkv, qkv, seg_col, seg_row, *before)


def attend_back(qkv, context, grad_context, lse, seg_col, seg_row, start, count):
    chunk = 256

    def kernel(q_ref, k_ref, v_ref, o_ref, g_ref, lse_ref, sc_ref, sr_ref, *rest):
        dq_ref, dk_ref, dv_ref, sum_ref, acc_ref, kt_ref = rest[-6:]
        lane = lax.broadcasted_iota(jnp.int32, (1, 2 * HD), 1)
        first = lane < HD
        q = q_ref[...] * jnp.asarray(SCALE, BF)
        g = g_ref[...]
        zero = jnp.zeros_like(q)
        prod = (g.astype(F32) * o_ref[...].astype(F32)).T
        inner = [jnp.sum(prod[h * HD : (h + 1) * HD], 0, keepdims=True) for h in range(2)]
        qm = [jnp.where(first, q, zero), jnp.where(first, zero, q)]
        gm = [jnp.where(first, g, zero), jnp.where(first, zero, g)]
        seg_q = sr_ref[...]
        kt_ref[...] = k_ref[...].T
        acc_ref[...] = jnp.zeros_like(acc_ref)
        sum_ref[1:2, :] = jnp.zeros((1, 2 * HD), F32)

        for c in range(SEQ // chunk):
            at = pl.ds(c * chunk, chunk)
            k = k_ref[at, :]
            v = v_ref[at, :]
            same = sc_ref[at, :] == seg_q
            dks, dvs = [], []
            for h in range(2):
                s = jnp.where(same, nt(k, qm[h]), MASKED)
                p = jnp.exp(s - lse_ref[0, h : h + 1, :])
                ds = (p * (nt(v, gm[h]) - inner[h])).astype(BF)
                dvs.append(nn(p.astype(BF), g))
                dks.append(nn(ds, q))
                half = pl.ds(h * HD, HD)
                acc_ref[half, :] += nn(kt_ref[half, at], ds)
            dk_ref[at, :] = jnp.where(first, dks[0], dks[1]).astype(BF)
            dv = jnp.where(first, dvs[0], dvs[1]).astype(BF)
            dv_ref[at, :] = dv
            sum_ref[1:2, :] += jnp.sum(dv.astype(F32), 0, keepdims=True)

        dq = (acc_ref[...].T * SCALE).astype(BF)
        dq_ref[...] = dq
        sum_ref[0:1, :] = jnp.sum(dq.astype(F32), 0, keepdims=True)

    spec = lambda off: pl.BlockSpec((SEQ, 2 * HD), lambda i: (0, i + off + start))
    full = lambda s: pl.BlockSpec(s, lambda i: (0,) * len(s))
    return pl.pallas_call(
        kernel,
        grid=(count,),
        in_specs=[spec(0), spec(PAIRS), spec(2 * PAIRS), spec(0), spec(0),
                  pl.BlockSpec((1, 8, SEQ), lambda i: (i + start, 0, 0)), full((SEQ, 1)),
                  full((1, SEQ))],
        out_specs=[pl.BlockSpec((SEQ, 2 * HD), lambda i: (0, i))] * 3
        + [pl.BlockSpec((8, 2 * HD), lambda i: (0, i))],
        out_shape=[jax.ShapeDtypeStruct((SEQ, 2 * HD * count), BF)] * 3
        + [jax.ShapeDtypeStruct((8, 2 * HD * count), F32)],
        scratch_shapes=[pltpu.VMEM((2 * HD, SEQ), F32), pltpu.VMEM((2 * HD, SEQ), BF)],
        compiler_params=params(),
        cost_estimate=cost(6 * count),
        name="attend_back",
    )(qkv, qkv, qkv, context, grad_context, lse, seg_col, seg_row)


def middle(me, context, x, g_own, g_near, vectors, up_bias, weight2, weight3, fsdp):
    _, refs2 = weight2
    _, refs3 = weight3
    count = copy_count(weight2)
    blocks = x.shape[0] // ROWS

    g_args, g_specs = own_and_near(g_own, g_near)

    def kernel(me_ref, c_ref, x_ref, vec_ref, ub_ref, *rest):
        g_refs, rest = rest[:blocks], rest[blocks:]
        w2, w3 = rest[: len(refs2)], rest[len(refs2) : len(refs2) + len(refs3)]
        o_refs = rest[len(refs2) + len(refs3) :][:blocks]
        (act_ref, gpre_ref, n1_ref, gffn_ref, gattn_ref, gres_ref, gctx_ref,
         sum_ref, usum_ref, wo, wu, wd, slope, g_ref, s_o, s_u, s_d) = rest[len(refs2) + len(refs3) + blocks :]
        step = pl.program_id(0)
        get_block(g_refs, step, g_ref)
        bits = bits_of(me_ref)
        co = weight_copies(weight2, w2, D // fsdp, (0, D // 2), (0, D), wo, s_o, bits)
        cu = weight_copies(weight2, w2, D // fsdp, (D // 2, FF // 2), (D, FF), wu, s_u, bits)
        cd = weight_copies(weight3, w3, FF // fsdp // 2, None, (0, D), wd, s_d, bits)

        @pl.when(step == 0)
        def _():
            start_all(co)
            start_all(cu)
            start_all(cd)
            sum_ref[...] = jnp.zeros_like(sum_ref)
            usum_ref[...] = jnp.zeros_like(usum_ref)
            wait_all(co)

        out_bias, gain1, shift1 = vec_ref[0:1], vec_ref[1:2], vec_ref[2:3]
        down_bias, gain2, shift2 = vec_ref[3:4], vec_ref[4:5], vec_ref[5:6]
        attn = nn(c_ref[...], wo[...]) + out_bias
        xhat1, rstd1 = norm_rows(x_ref[...].astype(F32) + attn)
        normed1 = xhat1 * gain1 + shift1
        low1 = normed1.astype(BF)
        n1_ref[...] = low1

        @pl.when(step == 0)
        def _():
            wait_all(cu)
            wait_all(cd)

        ffn = jnp.zeros((ROWS, D), F32)
        for lo in range(0, FF, D):
            at = slice(lo, lo + D)
            pre = nn(low1, wu[:, at]) + ub_ref[0:1, at]
            act, sl = gelu_with_slope(pre)
            act = act.astype(BF)
            act_ref[:, at] = act
            slope[:, at] = sl
            ffn = ffn + nn(act, wd[at, :])
        xhat2, rstd2 = norm_rows(normed1 + (ffn + down_bias))
        out = (xhat2 * gain2 + shift2).astype(BF)
        put_block(o_refs, step, out)
        gr = g_ref[...].astype(F32)
        res2 = norm_rows_back(gr * gain2, xhat2, rstd2)
        gffn = res2.astype(BF)
        gffn_ref[...] = gffn
        rs = lambda v: jnp.sum(v, 0, keepdims=True)
        sum_ref[0:1] += rs(gr * xhat2)
        sum_ref[1:2] += rs(gr)
        sum_ref[2:3] += rs(gffn.astype(F32))
        gn1 = res2
        for lo in range(0, FF, D):
            at = slice(lo, lo + D)
            gpre = (nt(gffn, wd[at, :]) * slope[:, at]).astype(BF)
            gpre_ref[:, at] = gpre
            usum_ref[0:1, at] += rs(gpre.astype(F32))
            gn1 = gn1 + nt(gpre, wu[:, at])
        sum_ref[3:4] += rs(gn1 * xhat1)
        sum_ref[4:5] += rs(gn1)
        res1 = norm_rows_back(gn1 * gain1, xhat1, rstd1)
        gres_ref[...] = res1
        gattn = res1.astype(BF)
        gattn_ref[...] = gattn
        sum_ref[5:6] += rs(gattn.astype(F32))
        gctx_ref[...] = nt(gattn, wo[...]).astype(BF)

    rows = x.shape[0]
    blk = lambda n: pl.BlockSpec((ROWS, n), lambda i, me: (i, 0))
    full = lambda s: pl.BlockSpec(s, lambda i, me: (0,) * len(s))
    sd = jax.ShapeDtypeStruct
    return pl.pallas_call(
        kernel,
        grid_spec=pltpu.PrefetchScalarGridSpec(
            num_scalar_prefetch=1,
            grid=(rows // ROWS,),
            in_specs=[blk(D), blk(D), full((8, D)), full((8, FF))] + g_specs
            + [ANY] * (len(refs2) + len(refs3)),
            out_specs=[full((ROWS, D))] * blocks + [blk(FF), blk(FF), blk(D), blk(D), blk(D), blk(D), blk(D),
                       full((8, D)), full((8, FF))],
            scratch_shapes=[
                pltpu.VMEM((D, D), BF), pltpu.VMEM((D, FF), BF), pltpu.VMEM((FF, D), BF),
                pltpu.VMEM((ROWS, FF), F32), pltpu.VMEM((ROWS, D), BF),
                pltpu.SemaphoreType.DMA((count,)), pltpu.SemaphoreType.DMA((count,)),
                pltpu.SemaphoreType.DMA((count,)),
            ],
        ),
        out_shape=[sd((ROWS, D), BF)] * blocks + [sd((rows, FF), BF), sd((rows, FF), BF), sd((rows, D), BF),
                   sd((rows, D), BF), sd((rows, D), BF), sd((rows, D), F32), sd((rows, D), BF),
                   sd((8, D), F32), sd((8, FF), F32)],
        compiler_params=params(),
        cost_estimate=cost(48),
        name="middle",
    )(me, context, x, vectors, up_bias, *g_args, *refs2, *refs3)


def nearness(d, me):
    x, z = lax.bitwise_xor(d & 1, me[1]), lax.bitwise_xor(d >> 1, me[2])
    return x, z


def grad_down(me, act, grad_ffn, fsdp, near):
    per = FF // fsdp
    steps = 8
    width = FF // steps
    inner = width // per
    assert inner == 1 or not near

    def kernel(me_ref, a_ref, g_ref, send_ref, keep_ref, acc_ref):
        core, _, _ = bits_of(me_ref)
        acc_ref[...] = tn(a_ref[...], g_ref[...])
        n = per // 2
        for i in range(inner):
            take = lambda b: acc_ref[pl.ds(pl.multiple_of(i * per + n * b, n), n), :].astype(BF)
            send_ref[i] = take(1 - core)
            keep_ref[i] = take(core)

    def where(i, me):
        if not near:
            return (i, 0, 0)
        x, z = nearness(i, me)
        return (x * (fsdp // 2) + z, 0, 0)

    rows = act.shape[0]
    out = jax.ShapeDtypeStruct((fsdp, per // 2, D), BF)
    ospec = pl.BlockSpec((inner, per // 2, D), where)
    return pl.pallas_call(
        kernel,
        grid_spec=pltpu.PrefetchScalarGridSpec(
            num_scalar_prefetch=1,
            grid=(steps,),
            in_specs=[pl.BlockSpec((rows, width), lambda i, me: (0, i)),
                      pl.BlockSpec((rows, D), lambda i, me: (0, 0))],
            out_specs=[ospec, ospec],
            scratch_shapes=[pltpu.VMEM((width, D), F32)],
        ),
        out_shape=[out, out],
        compiler_params=params(),
        cost_estimate=cost(12),
        name="grad_down",
    )(me, act, grad_ffn)


def write_half(step, moves, send_ref, keep_ref, sems):
    sending, keeping = (
        [pltpu.make_async_copy(a, b, sems.at[slot, i]) for i, (a, b) in enumerate(moves(slot, ref))]
        for slot, ref in enumerate((send_ref, keep_ref)))
    pl.when(step == 0)(lambda: start_all(sending))

    @pl.when(step == 1)
    def _():
        start_all(keeping)
        wait_all(sending)
        wait_all(keeping)


def half_of(i, core):
    return jnp.where(i == 0, 1 - core, core)


def grad_up_out(me, low1, grad_pre, context, grad_attn, fsdp, near):
    wu, wo = FF // 2, D // 2

    def kernel(me_ref, l_ref, p_ref, c_ref, a_ref, send_ref, keep_ref, slots, sems):
        step = pl.program_id(0)
        slots[step, :, :wo] = tn(c_ref[...], a_ref[...]).astype(BF)
        low = l_ref[...]
        for lo in range(0, wu, D):
            slots[step, :, wo + lo : wo + lo + D] = tn(low, p_ref[:, lo : lo + D]).astype(BF)

        def moves(slot, ref):
            if not near:
                return [(slots.at[slot], ref)]
            return [(slots.at[slot, pl.ds((2 * d + h) * n, n)],
                     ref.at[(lax.bitwise_xor(h, me_ref[0] >> 1),) + nearness(d, me_ref)])
                    for d in range(fsdp) for h in range(2)]

        write_half(step, moves, send_ref, keep_ref, sems)

    n = D // fsdp // 2
    count = 2 * fsdp if near else 1
    shape = (2, 2, fsdp // 2, n, wu + wo) if near else (D, wu + wo)
    rows = low1.shape[0]
    half = lambda n: pl.BlockSpec(
        (rows, n), lambda i, me: (0, half_of(i, lax.bitwise_and(me[0], 1))))
    full = pl.BlockSpec((rows, D), lambda i, me: (0, 0))
    return pl.pallas_call(
        kernel,
        grid_spec=pltpu.PrefetchScalarGridSpec(
            num_scalar_prefetch=1, grid=(2,),
            in_specs=[full, half(wu), full, half(wo)], out_specs=[ANY] * 2,
            scratch_shapes=[pltpu.VMEM((2, D, wu + wo), BF), pltpu.SemaphoreType.DMA((2, count))]),
        out_shape=[jax.ShapeDtypeStruct(shape, BF)] * 2,
        compiler_params=params(),
        cost_estimate=cost(12),
        name="grad_up_out",
    )(me, low1, grad_pre, context, grad_attn)


def grad_qkv(me, x, dqs, dks, dvs, sums, fsdp, near):
    parts = len(dqs)
    width = dqs[0].shape[1]
    group = width * parts
    w = 3 * group // 2
    per, per_up = D // fsdp, FF // fsdp
    tall = per + (SMALL if sums else 0)

    def kernel(me_ref, x_ref, *rest):
        q, k, v = (rest[i * parts : (i + 1) * parts] for i in range(3))
        sum_refs, (send_ref, keep_ref, slots, sems) = rest[3 * parts : -4], rest[-4:]
        core, _, _ = bits_of(me_ref)
        step = pl.program_id(0)
        b = half_of(step, core)

        def put(lo, ref, cols=slice(None)):
            val = tn(x_ref[...], ref[:, cols]).astype(BF)
            for d in range(fsdp):
                slots[step, d, :per, lo : lo + val.shape[1]] = val[d * per : (d + 1) * per]

        def put_half_k(second, lo):
            if parts == 1:
                put(lo, k[0], slice(width // 2 * second, width // 2 * (second + 1)))
            else:
                for i in range(parts // 2):
                    put(lo + i * width, k[parts // 2 * second + i])

        @pl.when(b == 0)
        def _():
            for i in range(parts):
                put(i * width, q[i])
            put_half_k(0, group)

        @pl.when(b == 1)
        def _():
            put_half_k(1, 0)
            for i in range(parts):
                put(group // 2 + i * width, v[i])

        if sums:
            s_ref, u_ref = sum_refs[:2]
            biases = jnp.concatenate([r[0:2] for r in sum_refs[2:]], 1)
            rows = jnp.concatenate([s_ref[0:6], biases], 0)
            for d in range(fsdp):
                slots[step, d, per:, :] = jnp.zeros((SMALL, w), BF)
                slots[step, d, per : per + 8, :per] = rows[:, d * per : (d + 1) * per].astype(BF)
                slots[step, d, per + 8 : per + 9, :per_up] = u_ref[0:1, d * per_up : (d + 1) * per_up].astype(BF)

        def moves(slot, ref):
            if not near:
                return [(slots.at[slot], ref)]
            return [(slots.at[slot, d], ref.at[nearness(d, me_ref)]) for d in range(fsdp)]

        write_half(step, moves, send_ref, keep_ref, sems)

    shape = (2, fsdp // 2, tall, w) if near else (fsdp, tall, w)
    full = lambda v: pl.BlockSpec(v.shape, lambda i, me: (0, 0))
    args = [x, *dqs, *dks, *dvs, *(sums or ())]
    return pl.pallas_call(
        kernel,
        grid_spec=pltpu.PrefetchScalarGridSpec(
            num_scalar_prefetch=1, grid=(2,),
            in_specs=[full(v) for v in args],
            out_specs=[ANY] * 2,
            scratch_shapes=[pltpu.VMEM((2, fsdp, tall, w), BF),
                            pltpu.SemaphoreType.DMA((2, fsdp if near else 1))]),
        out_shape=[jax.ShapeDtypeStruct(shape, BF)] * 2,
        compiler_params=params(),
        cost_estimate=cost(3 * parts),
        name="grad_qkv",
    )(me, *args)


def columns(mine, other, core, widths):
    zero = jnp.where(core == 0, mine, other)
    one = jnp.where(core == 0, other, mine)
    q, k, v = [], [], []
    lo = 0
    for n in widths:
        q.append(zero[..., lo : lo + n])
        k += [zero[..., lo + n : lo + 3 * n // 2], one[..., lo : lo + n // 2]]
        v.append(one[..., lo + n // 2 : lo + 3 * n // 2])
        lo += 3 * n // 2
    return jnp.concatenate(q + k + v, -1)


def grad_in(me, dqs, dks, dvs, res1, weight, fsdp):
    _, refs = weight
    n = 3 * D
    count = copy_count(weight)
    grads = [*dqs, *dks, *dvs]
    width = dqs[0].shape[1]

    def kernel(me_ref, *rest):
        g_refs, r_ref, rest = rest[: len(grads)], rest[len(grads)], rest[len(grads) + 1 :]
        w_refs, o_refs, (w_ref, sems) = rest[: len(refs)], rest[len(refs) : -2], rest[-2:]

        @pl.when(pl.program_id(0) == 0)
        def _():
            copies = weight_copies(weight, w_refs, D // fsdp, (0, n // 2), (0, n), w_ref, sems, bits_of(me_ref))
            start_all(copies)
            wait_all(copies)

        total = r_ref[...]
        for i, g in enumerate(g_refs):
            total = total + nt(g[...], w_ref[:, i * width : (i + 1) * width])
        put_block(o_refs, pl.program_id(0), total.astype(BF))

    rows = res1.shape[0]
    blocks = rows // ROWS
    blk = lambda c: pl.BlockSpec((ROWS, c), lambda i, me: (i, 0))
    return pl.pallas_call(
        kernel,
        grid_spec=pltpu.PrefetchScalarGridSpec(
            num_scalar_prefetch=1, grid=(blocks,),
            in_specs=[blk(width)] * len(grads) + [blk(D)] + [ANY] * len(refs),
            out_specs=[pl.BlockSpec((ROWS, D), lambda i, me: (0, 0))] * blocks,
            scratch_shapes=[pltpu.VMEM((D, n), BF), pltpu.SemaphoreType.DMA((count,))]),
        out_shape=[jax.ShapeDtypeStruct((ROWS, D), BF)] * blocks,
        compiler_params=params(),
        cost_estimate=cost(9),
        name="grad_in",
    )(me, *grads, res1, *refs)


def added(*parts):
    return sum(v.astype(F32) for v in parts).astype(BF)


def local(hidden_in, doc_starts, w_qkv, query_bias, value_bias, w_out, out_bias, norm1_gain,
          norm1_bias, w_up, up_bias, w_down, down_bias, norm2_gain, norm2_bias, cotangent):
    fsdp, sp = lax.axis_size("fsdp"), lax.axis_size("sp")
    seqs, span, _ = hidden_in.shape
    assert sp == 4 and seqs == sp and span * sp == SEQ and span == ROWS
    me = lax.axis_index("sp").astype(jnp.int32)
    core = me & 1
    row = lax.axis_index("fsdp").astype(jnp.int32)
    xb, zs = row & 1, fsdp // 2
    me1 = jnp.stack([me, xb, row >> 1])
    high = me >> 1
    rows_d, rows_f = D // fsdp, FF // fsdp
    split = in_pieces(fsdp)

    def partner(v, bit):
        return lax.ppermute(v, "sp", [(i, i ^ bit) for i in range(sp)])

    def away(v, bits):
        return lax.ppermute(v, "fsdp", [(i, i ^ bits) for i in range(fsdp)])

    def across(v):
        return away(v, 1)

    def swap(parts):
        two, three, one = [partner(parts[r - 1], r) for r in (2, 3, 1)]
        return [one, two, three]

    def fetch(v):
        return swap(deal(me1, v))

    def deliver(parts):
        parts = [parts[0]] + swap(parts[1:])
        return place(me1, parts)

    def half_cols(w):
        return lax.dynamic_slice(w, (0, core * (w.shape[1] // 2)), (w.shape[0], w.shape[1] // 2))

    def spread(v, groups):
        near = [v] + [away(v, 2 * z) for z in range(1, zs)]
        line = [near[g[0]] if len(g) == 1 else jnp.stack([near[z] for z in g]) for g in groups]
        line += [across(a) for a in line]
        return line + [partner(a, 1) for a in line]

    small = [out_bias, norm1_gain, norm1_bias, down_bias, norm2_gain, norm2_bias, query_bias,
             value_bias, up_bias]
    x_near = fetch(hidden_in)
    if split:
        weight1 = ("cols", spread(pack(me1, w_qkv, small), W1_GROUPS))
        table = None
        weight2 = ("cols", spread(jnp.concatenate([half_cols(w_out), half_cols(w_up)], 1), W2_GROUPS))
        down = lax.dynamic_slice(w_down, (core * (rows_f // 2), 0), (rows_f // 2, D))
        weight3 = ("rows", spread(down, W3_GROUPS))
    else:
        every = lax.all_gather(jnp.concatenate(small), "fsdp", axis=0).astype(F32)
        table = every[:, : 8 * rows_d].reshape(fsdp, 8, rows_d).transpose(1, 0, 2).reshape(8, D)
        full_up_bias = jnp.broadcast_to(every[:, 8 * rows_d :].reshape(1, FF), (8, FF))
        table = (table, full_up_bias)
        gather = lambda w: lax.all_gather(w, "fsdp", axis=0, tiled=True)
        weight1 = ("whole", (gather(w_qkv),))
        weight2 = ("whole", (gather(jnp.concatenate([w_out, w_up], 1)),))
        weight3 = ("whole", (gather(w_down),))
    g_near = fetch(cotangent)

    starts = lax.dynamic_slice(doc_starts, (me, 0), (1, doc_starts.shape[1]))
    order = jnp.arange(SEQ, dtype=jnp.int32)
    position = ((order // span) ^ me) * span + order % span
    seg = jnp.sum((position[:, None] >= starts).astype(jnp.int32), -1)
    seg_col, seg_row = seg[:, None], seg[None, :]

    qkv, x, table, full_up_bias = project(me1, hidden_in, x_near, weight1, table, fsdp)
    context = ()
    per = PAIRS // PARTS
    for i in range(PARTS):
        context = attend(qkv, seg_col, seg_row, i * per, per, context)
    context, lse = context
    (*out, act, gpre, low1, gffn, gattn, res1, gctx, sums, up_sums) = middle(
        me1, context, x, cotangent, g_near, table, full_up_bias, weight2, weight3, fsdp)
    layer_out = deliver(out)

    def join(mine, other, axis, bit=core):
        return jnp.where(bit == 0, jnp.concatenate([mine, other], axis),
                         jnp.concatenate([other, mine], axis))

    def finish(parts):
        near = [parts[0]] + [away(v, 2 * z) for z, v in enumerate(parts) if z]
        return added(*near)

    def reduce_part(send, keep):
        other = partner(send, 1)
        got = across(added(keep[1], other[1]))
        total = finish([added(keep[0, z], other[0, z], got[z]) for z in range(zs)])
        total = added(total, partner(total, 2))
        return total, partner(total, 1)

    def reduce_by_high(send, keep):
        other = partner(send, 1)
        got = partner(added(keep[1], other[1]), 2)
        far = across(added(keep[0, 1], other[0, 1], got[1]))
        total = finish([added(keep[0, 0, z], other[0, 0, z], got[0, z], far[z]) for z in range(zs)])
        total = join(total, partner(total, 2), 0, high)
        return total, partner(total, 1)

    def scatter(v):
        part = lax.psum_scatter(v, "fsdp", scatter_dimension=0, tiled=True)
        return lax.psum(part, "sp").astype(F32)

    down_parts = grad_down(me1, act, gffn, fsdp, split)
    wide_parts = grad_up_out(me1, low1, gpre, context, gattn, fsdp, split)
    if split:
        down = reduce_part(*[v.reshape((2, zs) + v.shape[1:]) for v in down_parts])
        wide = reduce_by_high(*wide_parts)
    dqs, dks, dvs, bias_sums = [], [], [], []
    widths, groups, halves = [], [], []
    for i in range(PARTS):
        dq, dk, dv, b = attend_back(qkv, context, gctx, lse, seg_col, seg_row, i * per, per)
        dqs, dks, dvs, bias_sums = dqs + [dq], dks + [dk], dvs + [dv], bias_sums + [b]
        if i in GROUP_ENDS:
            at = slice(sum(widths) // dq.shape[1], i + 1)
            widths.append((i + 1 - at.start) * dq.shape[1])
            extra = (sums, up_sums, *bias_sums) if i == PARTS - 1 else None
            halves.append(grad_qkv(me1, x, dqs[at], dks[at], dvs[at], extra, fsdp, split))
            if split:
                groups.append(reduce_part(*halves[-1]))
    dx = grad_in(me1, dqs, dks, dvs, res1, weight1, fsdp)
    grad_input = deliver(dx)

    if split:
        both = lambda pair, axis: join(pair[0], pair[1], axis).astype(F32)
        grad_down_w = both(down, 0)
        w1 = D // 2
        grad_out = both([v[:, :w1] for v in wide], 1)
        grad_up = both([v[:, w1:] for v in wide], 1)
        beside = [jnp.concatenate([v[i][:rows_d] for v in groups], -1) for i in range(2)]
        grad_q = columns(*beside, core, widths).astype(F32)
        tail = groups[-1][0][rows_d:].astype(F32)
        g2, b2, db, g1, b1, ob, qb, vb = [tail[i, :rows_d] for i in range(8)]
        ub = tail[8, :rows_f]
    else:
        grad_down_w = scatter(join(*down_parts[::-1], 1).reshape(FF, D).astype(F32))
        wide = scatter(join(*wide_parts[::-1], 1).astype(F32))
        w1, w2 = D // 2, FF // 2
        grad_out = jnp.concatenate([wide[:, :w1], wide[:, w1 + w2 : 2 * w1 + w2]], 1)
        grad_up = jnp.concatenate([wide[:, w1 : w1 + w2], wide[:, 2 * w1 + w2 :]], 1)
        sent, kept = [jnp.concatenate([h[i][:, :rows_d] for h in halves], -1) for i in range(2)]
        grad_q = scatter(columns(kept, sent, core, widths).reshape(D, 3 * D).astype(F32))
        by_dest = jnp.concatenate([sums[:6], jnp.concatenate([b[:2] for b in bias_sums], 1)], 0).reshape(8, fsdp, rows_d)
        by_dest = by_dest.transpose(1, 0, 2).reshape(fsdp, 8 * rows_d)
        extra = jnp.concatenate([by_dest, up_sums[0].reshape(fsdp, rows_f)], 1)
        tail = scatter(extra).reshape(-1)
        g2, b2, db, g1, b1, ob, qb, vb = [tail[i * rows_d : (i + 1) * rows_d] for i in range(8)]
        ub = tail[8 * rows_d :]
    return (layer_out, grad_input, grad_q, qb, vb, grad_out, ob, g1, b1, grad_up, ub, grad_down_w,
            db, g2, b2)


PARTS = 3
GROUP_ENDS = (1, 2)

W1_GROUPS = ((0,), (1,), (2,), (3,))
W2_GROUPS = ((0,), (1,), (2, 3))
W3_GROUPS = ((0,), (1, 2, 3))


def in_pieces(fsdp):
    return D // fsdp % 32 == 0 and FF // fsdp % 32 == 0


def solution(mesh):
    tok = P("fsdp", "sp", None)
    mat, vec = P("fsdp", None), P("fsdp")
    in_specs = (tok, mat, mat, vec, vec, mat, vec, vec, vec, mat, vec, mat, vec, vec, vec, tok)
    out_specs = (tok, tok, mat, vec, vec, mat, vec, vec, vec, mat, vec, mat, vec, vec, vec)

    return jax.shard_map(local, mesh=mesh, in_specs=in_specs, out_specs=out_specs, check_vma=False)
```
